512 devices in a mesh: firm: 32 (over x, y, z_hi), day: 16 (over z_lo, core).
Axes of the slice: x: 4, y: 4, z: 16 (z_hi: 2, z_lo: 8; z = z_hi * 8 + z_lo), core: 2. Of those that a mesh axis runs over, the one named last changes fastest.
Arguments:
- panel: float32 [65, 128, 16384], P(None, 'day', 'firm'), may hold values from -60 to 60, as said below
- presence: int32 [128, 16384], P(None, 'firm'), may hold values from 0 to 1, as said below
- firm_count: int32 [16384], P('firm'), may hold values from 1 to 128, as said below
- day_count: int32 [128], replicated, may hold values from 128 to 16384, as said below
Outputs:
- coefficients: float32 [64], replicated
- residual_panel: float32 [128, 16384], P('day', 'firm')
The draws below stay inside these ranges and needn't reach their ends.
Inputs may be any that keep to these rules, and one draw needn't show every extreme that they name: presence is 0 or 1; every firm has at least one entry and every day at least 128 entries; some firm is present on every day and some day holds every firm; presence rates differ strongly across firms and days. firm_count is the number of ones of presence in that firm's column. day_count is the number of ones of presence in that day's row. `panel`: values at absent entries are arbitrary and are not used.
All inputs are finite; a program needn't handle non-finite values.
Results may differ from the reference program's by a relative error of at most 0.00025.
Values sent between devices are 32-bit elements; how exact they have to be, the bound alone decides.
No kernel may reach another device: no remote copies, remote signals or barrier semaphores. Data moves between devices by JAX's collectives and lax.ppermute only.
A program may use at most 64 MiB of HBM per device.

```python
import jax
import jax.numpy as jnp
from jax import lax

K = 64
COLS = 65
SWEEPS = 3
FIRMS = 16384
DAYS = 128


def presence_table(key):
    base = jax.random.fold_in(key, 31)
    key_firm, key_day, key_draw = jax.random.split(base, 3)
    firm_rate = jax.random.randint(key_firm, (FIRMS,), 150, 951)
    day_rate = jax.random.randint(key_day, (DAYS,), 400, 1001)
    limit = day_rate[:, None] * firm_rate[None, :] // 1000
    integer_draw = jax.random.randint(key_draw, (DAYS, FIRMS), 0, 1000)
    day_index = lax.broadcasted_iota(jnp.int32, (DAYS, FIRMS), 0)
    firm_index = lax.broadcasted_iota(jnp.int32, (DAYS, FIRMS), 1)
    forced = (day_index == firm_index % DAYS) | (day_index == 0) | (firm_index == 0)
    return jnp.where((integer_draw < limit) | forced, 1, 0).astype(jnp.int32)


def draw_presence(key, part):
    return presence_table(key)


def draw_firm_count(key, part):
    return jnp.sum(presence_table(key), axis=0).astype(jnp.int32)


def draw_day_count(key, part):
    return jnp.sum(presence_table(key), axis=1).astype(jnp.int32)


def draw_panel(key, part):
    base = jax.random.fold_in(key, 57)
    keys = jax.random.split(base, 4)
    noise = jax.random.normal(keys[0], (COLS, DAYS, FIRMS), jnp.float32)
    firm_effect = jax.random.normal(keys[1], (COLS, 1, FIRMS), jnp.float32)
    day_effect = 0.7 * jax.random.normal(keys[2], (COLS, DAYS, 1), jnp.float32)
    regress = jnp.clip(noise + firm_effect + day_effect, -25.0, 25.0)
    slopes = 1.5 * jax.random.normal(keys[3], (K,), jnp.float32) / jnp.sqrt(K * 1.0)
    returns = jnp.tensordot(slopes, regress[:K], axes=1) + regress[K]
    returns = jnp.clip(returns, -55.0, 55.0)
    return jnp.concatenate([regress[:K], returns[None]], axis=0).astype(jnp.float32)


def setup_inputs(seed: int = 0) -> dict:
    seeds = jax.random.split(jax.random.key(seed), 5)
    panel = draw_panel(jax.random.fold_in(seeds[4], 71), 0)
    presence = draw_presence(jax.random.fold_in(seeds[4], 71), 0)
    firm_count = draw_firm_count(jax.random.fold_in(seeds[4], 71), 0)
    day_count = draw_day_count(jax.random.fold_in(seeds[4], 71), 0)
    return {"panel": panel, "presence": presence, "firm_count": firm_count, "day_count": day_count}


def sweep_column(column, mask_f, firm_n, day_n):
    current = column * mask_f
    for sweep in range(SWEEPS):
        firm_mean = jnp.sum(current, axis=0) / firm_n
        demeaned = mask_f * (current - firm_mean[None, :])
        day_mean = jnp.sum(demeaned, axis=1) / day_n
        current = mask_f * (demeaned - day_mean[:, None])
    return current

def reference(panel, presence, firm_count, day_count):
    mask_f = presence.astype(jnp.float32)
    firm_n = firm_count.astype(jnp.float32)
    day_n = day_count.astype(jnp.float32)
    demeaned = lax.map(lambda column: sweep_column(column, mask_f, firm_n, day_n), panel)
    flat = demeaned.reshape(demeaned.shape[0], -1)
    gram = jnp.dot(flat, flat.T, precision=lax.Precision.HIGHEST)
    matrix = gram[:K, :K]
    target = gram[:K, K:]
    factor = jnp.linalg.cholesky(matrix)
    middle = lax.linalg.triangular_solve(factor, target, left_side=True, lower=True)
    coefficients = lax.linalg.triangular_solve(factor, middle, left_side=True, lower=True, transpose_a=True)[:, 0]
    fitted = jnp.tensordot(coefficients, demeaned[:K], axes=1, precision=lax.Precision.HIGHEST)
    residual_panel = mask_f * (demeaned[K] - fitted)
    return (coefficients, residual_panel)
```

```python
import jax
import jax.numpy as jnp
from jax import lax
from jax.experimental import pallas as pl
from jax.experimental.pallas import tpu as pltpu
from jax.sharding import Mesh, PartitionSpec as P

K = 64
ROWS = 72
HIGHEST = lax.Precision.HIGHEST
F32 = jnp.float32


def iota(shape, axis):
    return lax.broadcasted_iota(jnp.int32, shape, axis)


def dot_t(a, b):
    return lax.dot_general(
        a, b, (((1,), (1,)), ((), ())), precision=HIGHEST, preferred_element_type=F32
    )


def dot(a, b):
    return lax.dot_general(
        a, b, (((1,), (0,)), ((), ())), precision=HIGHEST, preferred_element_type=F32
    )


def local_kernel(day_ref, panel_ref, pres_ref, msg_ref, gram_ref, rsum_ref):
    day = day_ref[0]
    mask = pres_ref[pl.ds(pl.multiple_of(day * 8, 8), 8), :].astype(F32)
    count = jnp.sum(mask, axis=0, keepdims=True)

    def column(t):
        tiles = []
        for j in range(4):
            target = panel_ref[32 * K + 8 * j + t : 32 * K + 8 * j + t + 1, :]
            regress = panel_ref[pl.ds(8 * j + t, K, stride=32), :]
            tiles.append(jnp.concatenate([regress, jnp.broadcast_to(target, (8, 128))], axis=0))
        return jnp.concatenate(tiles, axis=1)

    total = mask[0:1] * column(0)
    for t in range(1, 8):
        total = total + mask[t : t + 1] * column(t)
    for d in range(16):
        lanes = slice(32 * d, 32 * d + 32)
        msg_ref[d, 0:16, :] = jnp.concatenate(
            [total[16 * q : 16 * q + 16, lanes] for q in range(4)], axis=1
        )
        msg_ref[d, 16:24, :] = jnp.concatenate(
            [total[64:72, lanes], jnp.zeros((8, 96), F32)], axis=1
        )
    mean = total / jnp.maximum(count, 1.0)
    gram = jnp.zeros((ROWS, ROWS), F32)
    rsum = jnp.zeros((ROWS, 128), F32)
    lane = iota((ROWS, 128), 1)
    for t in range(8):
        centred = mask[t : t + 1] * (column(t) - mean)
        gram = gram + dot_t(centred, centred)
        sums = jnp.sum(centred, axis=1, keepdims=True)
        rsum = rsum + jnp.where(lane == 8 * day + t, sums, 0.0)
    gram_ref[...] = jnp.concatenate([gram, jnp.zeros((ROWS, 128 - ROWS), F32)], axis=1)
    rsum_ref[...] = rsum


def owner_kernel(day_ref, msg_ref, pres_ref, gram_ref, rsum_ref, pay_ref, mean_ref):
    day = day_ref[0]
    pick = (iota((512, 128), 0) == 32 * day + iota((512, 128), 1) % 32).astype(jnp.bfloat16)
    own = lax.dot_general(
        pres_ref[...].astype(F32).astype(jnp.bfloat16), pick, (((1,), (0,)), ((), ())),
        preferred_element_type=F32,
    )
    per_block = jnp.sum(own.reshape(16, 8, 128), axis=1)
    firm_n = jnp.sum(per_block, axis=0, keepdims=True)
    total = msg_ref[0]
    for b in range(1, 16):
        total = total + msg_ref[b]
    mean = total / firm_n
    delta = [msg_ref[b] / jnp.maximum(per_block[b : b + 1], 1.0) - mean for b in range(16)]

    def unpack(parts):
        rows = [
            jnp.concatenate([p[0:16, 32 * q : 32 * q + 32] for p in parts], axis=1)
            for q in range(4)
        ]
        rows.append(jnp.concatenate([p[16:24, 0:32] for p in parts], axis=1))
        return jnp.concatenate(rows, axis=0)

    mean_ref[...] = unpack([mean] * 4)
    gram = gram_ref[:, 0:ROWS]
    rsum = rsum_ref[...]
    block = iota((128, 128), 0) // 8
    group = iota((128, 128), 1) // 32
    for j in range(4):
        spread = unpack(delta[4 * j : 4 * j + 4])
        cells = jnp.where(block == 4 * j + group, own, 0.0)
        weight = jnp.sum(cells, axis=0, keepdims=True)
        gram = gram + dot_t(spread * weight, spread)
        rsum = rsum + dot_t(spread, cells)
    weight = jnp.where(iota((1, 128), 1) < 32, 1.0 / firm_n, 0.0)
    pay_ref[128:256, :] = dot_t(own * weight, own)
    pay_ref[0:64, :] = rsum[0:64]
    ret = rsum[64:72]
    row = iota((8, 128), 0)
    extra = jnp.where(
        row == 0,
        pltpu.roll(ret, 65, 1),
        jnp.where(row == 1, pltpu.roll(ret, 2, 1), jnp.where(row == 2, pltpu.roll(ret, 67, 1), 0.0)),
    )
    wide = jnp.concatenate([gram[0:64], jnp.zeros((64, 128 - ROWS), F32)], axis=1)
    extra = jnp.concatenate([extra, jnp.zeros((56, 128), F32)], axis=0)
    pay_ref[64:128, :] = jnp.where(iota((64, 128), 1) < 65, wide, extra)


def solve_kernel(day_ref, pay_ref, dayn_ref, mean_ref, w_ref, days_ref, firm_ref):
    day = day_ref[0]
    head = pay_ref[64:72, :]
    lane8 = iota((8, 128), 1)
    ret = jnp.where(
        lane8[0:1] < 63,
        pltpu.roll(head, 63, 1)[0:1],
        jnp.where(lane8[0:1] < 126, pltpu.roll(head, 126, 1)[1:2], pltpu.roll(head, 61, 1)[2:3]),
    )
    r = jnp.concatenate([pay_ref[0:64, :], jnp.broadcast_to(ret, (8, 128))], axis=0)
    cross = pay_ref[128:256, :]
    n = dayn_ref[...].astype(F32)
    d1 = r / n
    q1 = dot(d1, cross)
    d2 = q1 / n
    q2 = dot(d2, cross)
    d3 = q2 / n
    taken = dot_t(
        jnp.concatenate([r, q1, q2], axis=1), jnp.concatenate([d1 + d2, d2 + d3, d3], axis=1)
    )
    a = pay_ref[64:128, 0:ROWS] - taken[0:64, :]
    rowid = iota((64, ROWS), 0)
    for k in range(K):
        scaled = a[k : k + 1, :] / a[k : k + 1, k : k + 1]
        a = jnp.where(rowid == k, scaled, a - a[:, k : k + 1] * scaled)
    coef = a[:, 64:65]
    w = jnp.concatenate([-coef, (iota((8, 1), 0) == 0).astype(F32)], axis=0)
    w_ref[...] = jnp.sum(
        jnp.where(iota((ROWS, 128), 0) == iota((ROWS, 128), 1), w, 0.0), axis=0, keepdims=True
    )
    e = d1 + d2
    ew = jnp.sum(w * e, axis=0, keepdims=True)
    dw = jnp.sum(w * (e + d3), axis=0, keepdims=True)
    days_ref[...] = jnp.concatenate([ew, dw, jnp.zeros((6, 128), F32)], axis=0)
    fw = jnp.sum(w * mean_ref[...], axis=0, keepdims=True)
    firm_ref[...] = jnp.where(lane8[0:1] // 32 == day % 4, fw, 0.0)


def residual_kernel(day_ref, w_ref, panel_ref, pres_ref, firmn_ref, days_ref, firm_ref, out_ref):
    day = day_ref[0]
    mask = pres_ref[pl.ds(pl.multiple_of(day * 8, 8), 8), :].astype(F32)
    acc = panel_ref[32 * K : 32 * K + 32, :]
    for c in range(K):
        acc = acc + w_ref[0, c] * panel_ref[32 * c : 32 * c + 32, :]
    acc = jnp.concatenate([acc[8 * j : 8 * j + 8] for j in range(4)], axis=1)
    firm = jnp.concatenate(
        [jnp.sum(firm_ref[4 * j : 4 * j + 4, :], axis=0, keepdims=True) for j in range(4)], axis=1
    )
    days = days_ref[...]
    back = dot(days, pres_ref[...].astype(F32))[0:1]
    firm = back / firmn_ref[...].astype(F32) - firm
    here = iota((8, 128), 1) == 8 * day + iota((8, 128), 0)
    dw = jnp.sum(jnp.where(here, days[1:2], 0.0), axis=1, keepdims=True)
    out_ref[...] = mask * (acc + firm - dw)


def call(kernel, out, smem, *args):
    spaces = [pltpu.SMEM if i < smem else pltpu.VMEM for i in range(len(args))]
    return pl.pallas_call(
        kernel,
        out_shape=[jax.ShapeDtypeStruct(s, F32) for s in out],
        in_specs=[pl.BlockSpec(memory_space=s) for s in spaces],
        out_specs=[pl.BlockSpec(memory_space=pltpu.VMEM) for _ in out],
        name=kernel.__name__,
    )(*args)


def exchange(x, axes):
    return lax.all_to_all(x, axes, 0, 0, tiled=True)


def on_device(panel, presence, firm_count, day_count):
    day = lax.axis_index(("z", "c")).astype(jnp.int32).reshape(1)
    panel = panel.reshape(65, 8, 4, 128).transpose(0, 2, 1, 3).reshape(65 * 32, 128)
    msg, gram, rsum = call(
        local_kernel, [(16, 24, 128), (ROWS, 128), (ROWS, 128)], 1, day, panel, presence
    )
    msg = exchange(msg, ("z", "c"))
    pay, mean = call(owner_kernel, [(256, 128), (ROWS, 128)], 1, day, msg, presence, gram, rsum)
    pay = exchange(pay.reshape(32, 8, 128), ("x", "y", "c"))
    pay = jnp.broadcast_to(jnp.sum(pay, axis=0)[None], (16, 8, 128))
    pay = exchange(pay, ("h", "z"))
    pay = jnp.broadcast_to(jnp.sum(pay, axis=0)[None], (32, 8, 128))
    pay = exchange(pay, ("x", "y", "c")).reshape(256, 128)
    w, days, firm = call(
        solve_kernel, [(1, 128), (8, 128), (1, 128)], 1, day, pay, day_count.reshape(1, 128), mean
    )
    firm = exchange(jnp.broadcast_to(firm[None], (16, 1, 128)), ("z", "c")).reshape(16, 128)
    (residual,) = call(
        residual_kernel, [(8, 512)], 2, day, w, panel, presence, firm_count.reshape(1, 512), days, firm
    )
    return -w[0, :K], residual


def solution(mesh):
    split = Mesh(mesh.devices.reshape(4, 4, 2, 8, 2), ("x", "y", "h", "z", "c"))
    firm, day = ("x", "y", "h"), ("z", "c")
    return jax.shard_map(
        on_device,
        mesh=split,
        in_specs=(P(None, day, firm), P(None, firm), P(firm), P()),
        out_specs=(P(), P(day, firm)),
        check_vma=False,
    )
```

```python
import jax
import jax.numpy as jnp
from jax import lax
from jax.experimental import pallas as pl
from jax.experimental.pallas import tpu as pltpu
from jax.sharding import Mesh, PartitionSpec as P

K = 64
ROWS = 72
HIGHEST = lax.Precision.HIGHEST
F32 = jnp.float32


def iota(shape, axis):
    return lax.broadcasted_iota(jnp.int32, shape, axis)


def dot_t(a, b):
    return lax.dot_general(
        a, b, (((1,), (1,)), ((), ())), precision=HIGHEST, preferred_element_type=F32
    )


def dot(a, b):
    return lax.dot_general(
        a, b, (((1,), (0,)), ((), ())), precision=HIGHEST, preferred_element_type=F32
    )


def stacked(panel_ref, t):
    tiles = []
    for j in range(4):
        row = 8 * j + t
        target = panel_ref[32 * K + row : 32 * K + row + 1, :]
        regress = panel_ref[pl.ds(row, K, stride=32), :]
        tiles.append(jnp.concatenate([regress, jnp.broadcast_to(target, (8, 128))], axis=0))
    return jnp.concatenate(tiles, axis=1)


def sums_kernel(day_ref, panel_hbm, pres_hbm, msg_ref, panel_ref, pres_ref, sems):
    start = pl.multiple_of(day_ref[0] * 8, 8)
    copies = [pltpu.make_async_copy(pres_hbm.at[pl.ds(start, 8), :], pres_ref, sems.at[0])]
    pieces = [slice(512 * q, 512 * q + 512) for q in range(4)] + [slice(32 * K, 32 * K + 32)]
    for i, rows in enumerate(pieces):
        copies.append(
            pltpu.make_async_copy(panel_hbm.at[rows, :], panel_ref.at[rows, :], sems.at[i + 1])
        )
    for copy in copies:
        copy.start()
    copies[0].wait()
    mask = pres_ref[...].astype(F32)
    for q in range(4):
        copies[q + 1].wait()
        tiles = []
        for j in range(4):
            total = None
            for t in range(8):
                x = panel_ref[pl.ds(512 * q + 8 * j + t, 16, stride=32), :]
                x = x * mask[t : t + 1, 128 * j : 128 * j + 128]
                total = x if total is None else total + x
            tiles.append(total)
        for d in range(16):
            lanes = slice(32 * (d % 4), 32 * (d % 4) + 32)
            msg_ref[17 * d : 17 * d + 16, 32 * q : 32 * q + 32] = tiles[d // 4][:, lanes]
    copies[5].wait()
    for j in range(4):
        x = panel_ref[32 * K + 8 * j : 32 * K + 8 * j + 8, :] * mask[:, 128 * j : 128 * j + 128]
        total = jnp.sum(x, axis=0, keepdims=True)
        for s in range(4):
            d = 4 * j + s
            msg_ref[17 * d + 16 : 17 * d + 17, :] = jnp.zeros((1, 128), F32)
            msg_ref[17 * d + 16 : 17 * d + 17, 0:32] = total[:, 32 * s : 32 * s + 32]


def scatter_kernel(day_ref, panel_ref, pres_ref, gram_ref, rsum_ref, own_ref, cross_ref):
    day = day_ref[0]
    mask = pres_ref[pl.ds(pl.multiple_of(day * 8, 8), 8), :].astype(F32)
    count = jnp.sum(mask, axis=0, keepdims=True)
    total = mask[0:1] * stacked(panel_ref, 0)
    for t in range(1, 8):
        total = total + mask[t : t + 1] * stacked(panel_ref, t)
    mean = total / jnp.maximum(count, 1.0)
    gram = jnp.zeros((ROWS, ROWS), F32)
    rsum = jnp.zeros((ROWS, 128), F32)
    lane = iota((ROWS, 128), 1)
    for t in range(8):
        centred = mask[t : t + 1] * (stacked(panel_ref, t) - mean)
        gram = gram + dot_t(centred, centred)
        sums = jnp.sum(centred, axis=1, keepdims=True)
        rsum = rsum + jnp.where(lane == 8 * day + t, sums, 0.0)
    gram_ref[...] = jnp.concatenate([gram, jnp.zeros((ROWS, 128 - ROWS), F32)], axis=1)
    rsum_ref[...] = rsum
    pick = (iota((512, 128), 0) == 32 * day + iota((512, 128), 1) % 32).astype(jnp.bfloat16)
    own = lax.dot_general(
        pres_ref[...].astype(F32).astype(jnp.bfloat16), pick, (((1,), (0,)), ((), ())),
        preferred_element_type=F32,
    )
    own_ref[...] = own
    firm_n = jnp.sum(own, axis=0, keepdims=True)
    weight = jnp.where(iota((1, 128), 1) < 32, 1.0 / firm_n, 0.0)
    cross_ref[...] = dot_t(own * weight, own)


def owner_kernel(msg_ref, gram_ref, rsum_ref, own_ref, cross_ref, pay_ref, mean_ref):
    own = own_ref[...]
    per_block = jnp.sum(own.reshape(16, 8, 128), axis=1)
    firm_n = jnp.sum(per_block, axis=0, keepdims=True)
    msg = [msg_ref[17 * b : 17 * b + 16, :] for b in range(16)]
    last = jnp.concatenate([msg_ref[17 * b + 16 : 17 * b + 17, :] for b in range(16)], axis=0)
    total = msg[0]
    for b in range(1, 16):
        total = total + msg[b]
    mean = total / firm_n
    last_mean = jnp.sum(last, axis=0, keepdims=True) / firm_n
    mean_ref[0:16, :] = mean
    mean_ref[16:17, :] = last_mean
    held = jnp.maximum(per_block, 1.0)
    delta = [msg[b] / held[b : b + 1] - mean for b in range(16)]
    last = last / held - last_mean

    gram = gram_ref[:, 0:ROWS]
    rsum = rsum_ref[...]
    block = iota((128, 128), 0) // 8
    group = iota((128, 128), 1) // 32
    for j in range(4):
        rows = [
            jnp.concatenate([delta[4 * j + s][:, 32 * q : 32 * q + 32] for s in range(4)], axis=1)
            for q in range(4)
        ]
        ret = jnp.concatenate([last[4 * j + s : 4 * j + s + 1, 0:32] for s in range(4)], axis=1)
        rows.append(jnp.broadcast_to(ret, (8, 128)))
        spread = jnp.concatenate(rows, axis=0)
        cells = jnp.where(block == 4 * j + group, own, 0.0)
        weight = jnp.sum(cells, axis=0, keepdims=True)
        gram = gram + dot_t(spread * weight, spread)
        rsum = rsum + dot_t(spread, cells)
    pay_ref[128:256, :] = cross_ref[...]
    pay_ref[0:64, :] = rsum[0:64]
    ret = rsum[64:72]
    row = iota((8, 128), 0)
    extra = jnp.where(
        row == 0,
        pltpu.roll(ret, 65, 1),
        jnp.where(row == 1, pltpu.roll(ret, 2, 1), jnp.where(row == 2, pltpu.roll(ret, 67, 1), 0.0)),
    )
    wide = jnp.concatenate([gram[0:64], jnp.zeros((64, 128 - ROWS), F32)], axis=1)
    extra = jnp.concatenate([extra, jnp.zeros((56, 128), F32)], axis=0)
    pay_ref[64:128, :] = jnp.where(iota((64, 128), 1) < 65, wide, extra)


def eliminate(a):
    rowid = iota((64, 128), 0)
    for k in range(0, K, 4):
        cols = [jnp.broadcast_to(a[:, k + j : k + j + 1], (64, 128)) for j in range(4)]
        rows = [a[k + i : k + i + 1, :] for i in range(4)]
        block = [[cols[j][k + i : k + i + 1, :] for j in range(4)] for i in range(4)]
        for i in range(4):
            inverse = 1.0 / block[i][i]
            rows[i] = rows[i] * inverse
            for j in range(i + 1, 4):
                block[i][j] = block[i][j] * inverse
            for m in range(4):
                if m != i:
                    rows[m] = rows[m] - block[m][i] * rows[i]
                    for j in range(i + 1, 4):
                        block[m][j] = block[m][j] - block[m][i] * block[i][j]
        rest = a
        for i in range(4):
            rest = rest - cols[i] * rows[i]
        for i in range(4):
            rest = jnp.where(rowid == k + i, rows[i], rest)
        a = rest
    return a


def solve_kernel(
    day_ref, side_ref, panel_hbm, pay_ref, dayn_ref, near_ref, far_ref, pres_ref, firmn_ref,
    coef_ref, out_ref, panel_ref, w_ref, sem,
):
    copy = pltpu.make_async_copy(panel_hbm, panel_ref, sem)
    copy.start()
    day = day_ref[0]
    lane = iota((1, 128), 1)
    head = pay_ref[64:72, :]
    ret = jnp.where(
        lane < 63,
        pltpu.roll(head, 63, 1)[0:1],
        jnp.where(lane < 126, pltpu.roll(head, 126, 1)[1:2], pltpu.roll(head, 61, 1)[2:3]),
    )
    r = jnp.concatenate([pay_ref[0:64, :], jnp.broadcast_to(ret, (8, 128))], axis=0)
    cross = pay_ref[128:256, :]
    n = dayn_ref[...].astype(F32)
    d1 = r / n
    q1 = dot(d1, cross)
    d2 = q1 / n
    q2 = dot(d2, cross)
    d3 = q2 / n
    right = jnp.concatenate([d1 + d2, d2 + d3, d3], axis=1)
    right = jnp.concatenate([right, jnp.zeros((128 - ROWS, 384), F32)], axis=0)
    left = jnp.concatenate([r[0:64], q1[0:64], q2[0:64]], axis=1)
    solved = eliminate(pay_ref[64:128, :] - dot_t(left, right))
    coef = jnp.broadcast_to(solved[:, 64:65], (64, 128))
    picked = jnp.where(iota((64, 128), 0) == iota((64, 128), 1), coef, 0.0)
    coef_ref[...] = jnp.sum(picked, axis=0, keepdims=True)[:, 0:K]
    w = jnp.concatenate([-coef, (iota((8, 128), 0) == 0).astype(F32)], axis=0)
    w_ref[...] = w
    e = d1 + d2
    ew = jnp.sum(w * e, axis=0, keepdims=True)
    dw = jnp.sum(w * (e + d3), axis=0, keepdims=True)
    back = dot(jnp.broadcast_to(ew, (8, 128)), pres_ref[...].astype(F32))[0:1]
    here = iota((8, 128), 1) == 8 * day + iota((8, 128), 0)
    dw = jnp.sum(jnp.where(here, dw, 0.0), axis=1, keepdims=True)
    packed = jnp.zeros((16, 128), F32)
    for q in range(4):
        packed = jnp.where(iota((16, 128), 1) // 32 == q, w[16 * q : 16 * q + 16], packed)
    core = day % 2
    first = 25 * 8 * side_ref[0]

    def part(ref, z):
        row = first + 25 * z + 8
        one = jnp.sum(packed * ref[pl.ds(row, 16), :], axis=0, keepdims=True)
        return one + jnp.where(lane < 32, ref[pl.ds(row + 16, 1), :], 0.0)

    parts = []
    for z in range(8):
        mine, theirs = part(near_ref, z), part(far_ref, z)
        parts += [jnp.where(core == 0, mine, theirs), jnp.where(core == 0, theirs, mine)]
    parts = jnp.concatenate(parts, axis=0)
    parts = parts + pltpu.roll(parts, 32, 1)
    parts = parts + pltpu.roll(parts, 64, 1)
    parts = jnp.where(iota((16, 128), 1) // 32 == iota((16, 128), 0) % 4, parts, 0.0)
    firm = jnp.concatenate(
        [jnp.sum(parts[4 * j : 4 * j + 4], axis=0, keepdims=True) for j in range(4)], axis=1
    )
    firm = back / firmn_ref[...].astype(F32) - firm
    mask = pres_ref[pl.ds(pl.multiple_of(day * 8, 8), 8), :].astype(F32)
    copy.wait()
    acc = panel_ref[32 * K : 32 * K + 32, :]
    for c in range(K):
        weight = jnp.broadcast_to(w_ref[c : c + 1, :], (32, 128))
        acc = acc + weight * panel_ref[32 * c : 32 * c + 32, :]
    acc = jnp.concatenate([acc[8 * j : 8 * j + 8] for j in range(4)], axis=1)
    out_ref[...] = mask * (acc + firm - dw)


def call(kernel, out, spaces, scratch, *args):
    kinds = {"s": pltpu.SMEM, "v": pltpu.VMEM, "p": pltpu.VMEM, "h": pl.ANY}
    args = [
        pltpu.with_memory_space_constraint(a, pltpu.VMEM) if s == "v" else a
        for s, a in zip(spaces, args)
    ]
    return pl.pallas_call(
        kernel,
        out_shape=[pltpu.VMEM(s, F32) if v else jax.ShapeDtypeStruct(s, F32) for s, v in out],
        in_specs=[pl.BlockSpec(memory_space=kinds[s]) for s in spaces],
        out_specs=[pl.BlockSpec(memory_space=pltpu.VMEM) for _ in out],
        scratch_shapes=scratch,
        name=kernel.__name__,
    )(*args)


PANEL = pltpu.VMEM((65 * 32, 128), F32)


def sums(day, panel, presence):
    scratch = [PANEL, pltpu.VMEM((8, 512), jnp.int32), pltpu.SemaphoreType.DMA((6,))]
    return call(sums_kernel, [((272, 128), True)], "shh", scratch, day, panel, presence)[0]


def scatter(day, panel, presence):
    shapes = [((n, 128), True) for n in (ROWS, ROWS, 128, 128)]
    return call(scatter_kernel, shapes, "spp", [], day, panel, presence)


def owner(*args):
    return call(owner_kernel, [((256, 128), True), ((17, 128), True)], "vvvvv", [], *args)


def solve(day, side, panel, pay, day_n, near, far, presence, firm_n):
    scratch = [PANEL, pltpu.VMEM((ROWS, 128), F32), pltpu.SemaphoreType.DMA]
    return call(
        solve_kernel, [((1, K), False), ((8, 512), False)], "sshvpvvpp", scratch,
        day, side, panel, pay, day_n, near, far, presence, firm_n,
    )


def exchange(x, axes):
    return lax.all_to_all(x, axes, 0, 0, tiled=True)


def on_device(panel, presence, firm_count, day_count):
    day = lax.axis_index(("z", "c")).astype(jnp.int32).reshape(1)
    side = lax.axis_index("h").astype(jnp.int32).reshape(1)
    panel = panel.reshape(65, 8, 4, 128).transpose(0, 2, 1, 3).reshape(65 * 32, 128)
    msg = exchange(sums(day, panel, presence).reshape(16, 1, 17 * 128), ("z", "c"))
    here = scatter(day, panel, presence)
    pay, mean = owner(msg.reshape(272, 128), *here)
    pay = jnp.sum(exchange(pay.reshape(32, 8, 128), ("x", "y", "c")), axis=0)
    near = jnp.concatenate([pay.reshape(1, 1, 8 * 128), mean.reshape(1, 1, 17 * 128)], axis=2)
    near = exchange(jnp.broadcast_to(near, (16, 1, 25 * 128)), ("h", "z"))
    far = lax.ppermute(near, "c", ((0, 1), (1, 0)))
    pay = jnp.sum(near[:, 0, : 8 * 128], axis=0).reshape(8, 128)
    pay = exchange(jnp.broadcast_to(pay[None], (32, 8, 128)), ("x", "y", "c")).reshape(256, 128)
    near, far = near.reshape(400, 128), far.reshape(400, 128)
    coef, residual = solve(
        day, side, panel, pay, day_count.reshape(1, 128), near, far, presence,
        firm_count.reshape(1, 512),
    )
    return coef.reshape(K), residual


def solution(mesh):
    split = Mesh(mesh.devices.reshape(4, 4, 2, 8, 2), ("x", "y", "h", "z", "c"))
    firm, day = ("x", "y", "h"), ("z", "c")
    return jax.shard_map(
        on_device,
        mesh=split,
        in_specs=(P(None, day, firm), P(None, firm), P(firm), P()),
        out_specs=(P(), P(day, firm)),
        check_vma=False,
    )
```

```python
import jax
import jax.numpy as jnp
from jax import lax
from jax.experimental import pallas as pl
from jax.experimental.pallas import tpu as pltpu
from jax.sharding import Mesh, PartitionSpec as P

K = 64
ROWS = 72
HIGHEST = lax.Precision.HIGHEST
F32 = jnp.float32


def iota(shape, axis):
    return lax.broadcasted_iota(jnp.int32, shape, axis)


def dot_t(a, b):
    return lax.dot_general(
        a, b, (((1,), (1,)), ((), ())), precision=HIGHEST, preferred_element_type=F32
    )


def dot(a, b):
    return lax.dot_general(
        a, b, (((1,), (0,)), ((), ())), precision=HIGHEST, preferred_element_type=F32
    )


def stacked(panel_ref, t):
    tiles = []
    for j in range(4):
        row = 8 * j + t
        target = panel_ref[32 * K + row : 32 * K + row + 1, :]
        regress = panel_ref[pl.ds(row, K, stride=32), :]
        tiles.append(jnp.concatenate([regress, jnp.broadcast_to(target, (8, 128))], axis=0))
    return jnp.concatenate(tiles, axis=1)


def sums_kernel(day_ref, panel_hbm, pres_hbm, msg_ref, panel_ref, pres_ref, sems):
    start = pl.multiple_of(day_ref[0] * 8, 8)
    copies = [pltpu.make_async_copy(pres_hbm.at[pl.ds(start, 8), :], pres_ref, sems.at[0])]
    pieces = [slice(512 * q, 512 * q + 512) for q in range(4)] + [slice(32 * K, 32 * K + 32)]
    for i, rows in enumerate(pieces):
        copies.append(
            pltpu.make_async_copy(panel_hbm.at[rows, :], panel_ref.at[rows, :], sems.at[i + 1])
        )
    for copy in copies:
        copy.start()
    copies[0].wait()
    mask = pres_ref[...].astype(F32)
    low = [iota((8, 128), 0) % (2 * n) < n for n in (4, 2, 1)]
    for q in range(4):
        copies[q + 1].wait()
        tiles = []
        for j in range(4):
            held = mask[:, 128 * j : 128 * j + 128]
            halves = []
            for half in range(2):
                base = 512 * q + 256 * half + 8 * j
                rows = [base + 32 * c for c in (0, 4, 2, 6, 1, 5, 3, 7)]
                level = [panel_ref[r : r + 8, :] * held for r in rows]
                for n, mine in zip((4, 2, 1), low):
                    level = [
                        jnp.where(mine, x + pltpu.roll(x, 8 - n, 0), y + pltpu.roll(y, n, 0))
                        for x, y in zip(level[0::2], level[1::2])
                    ]
                halves.append(level[0])
            tiles.append(jnp.concatenate(halves, axis=0))
        for d in range(16):
            lanes = slice(32 * (d % 4), 32 * (d % 4) + 32)
            msg_ref[17 * d : 17 * d + 16, 32 * q : 32 * q + 32] = tiles[d // 4][:, lanes]
    copies[5].wait()
    for j in range(4):
        x = panel_ref[32 * K + 8 * j : 32 * K + 8 * j + 8, :] * mask[:, 128 * j : 128 * j + 128]
        total = jnp.sum(x, axis=0, keepdims=True)
        for s in range(4):
            d = 4 * j + s
            msg_ref[17 * d + 16 : 17 * d + 17, :] = jnp.zeros((1, 128), F32)
            msg_ref[17 * d + 16 : 17 * d + 17, 0:32] = total[:, 32 * s : 32 * s + 32]


def scatter_kernel(
    day_ref, panel_ref, pres_ref, dayn_ref, gram_ref, rsum_ref, own_ref, cross_ref, mask_ref, count_ref
):
    day = day_ref[0]
    every = pres_ref[...].astype(F32)
    mask_ref[...] = every
    firm_n = jnp.sum(every, axis=0, keepdims=True)
    day_n = jnp.concatenate([dayn_ref[...].astype(F32), jnp.zeros((1, 384), F32)], axis=1)
    count_ref[...] = jnp.concatenate([firm_n, day_n, jnp.zeros((6, 512), F32)], axis=0)
    mask = mask_ref[pl.ds(pl.multiple_of(day * 8, 8), 8), :]
    count = jnp.sum(mask, axis=0, keepdims=True)
    total = mask[0:1] * stacked(panel_ref, 0)
    for t in range(1, 8):
        total = total + mask[t : t + 1] * stacked(panel_ref, t)
    mean = total / jnp.maximum(count, 1.0)
    gram = jnp.zeros((ROWS, ROWS), F32)
    rsum = jnp.zeros((ROWS, 128), F32)
    lane = iota((ROWS, 128), 1)
    for t in range(8):
        centred = mask[t : t + 1] * (stacked(panel_ref, t) - mean)
        gram = gram + dot_t(centred, centred)
        sums = jnp.sum(centred, axis=1, keepdims=True)
        rsum = rsum + jnp.where(lane == 8 * day + t, sums, 0.0)
    gram_ref[...] = jnp.concatenate([gram, jnp.zeros((ROWS, 128 - ROWS), F32)], axis=1)
    rsum_ref[...] = rsum
    pick = (iota((512, 128), 0) == 32 * day + iota((512, 128), 1) % 32).astype(jnp.bfloat16)
    own = lax.dot_general(
        every.astype(jnp.bfloat16), pick, (((1,), (0,)), ((), ())),
        preferred_element_type=F32,
    )
    own_ref[...] = own
    firm_n = jnp.sum(own, axis=0, keepdims=True)
    weight = jnp.where(iota((1, 128), 1) < 32, 1.0 / firm_n, 0.0)
    cross_ref[...] = dot_t(own * weight, own)


def owner_kernel(msg_ref, gram_ref, rsum_ref, own_ref, cross_ref, pay_ref, mean_ref):
    own = own_ref[...]
    per_block = jnp.sum(own.reshape(16, 8, 128), axis=1)
    firm_n = jnp.sum(per_block, axis=0, keepdims=True)
    msg = [msg_ref[17 * b : 17 * b + 16, :] for b in range(16)]
    last = jnp.concatenate([msg_ref[17 * b + 16 : 17 * b + 17, :] for b in range(16)], axis=0)
    total = msg[0]
    for b in range(1, 16):
        total = total + msg[b]
    mean = total / firm_n
    last_mean = jnp.sum(last, axis=0, keepdims=True) / firm_n
    mean_ref[0:16, :] = mean
    mean_ref[16:17, :] = last_mean
    held = jnp.maximum(per_block, 1.0)
    delta = [msg[b] / held[b : b + 1] - mean for b in range(16)]
    last = last / held - last_mean

    gram = gram_ref[:, 0:ROWS]
    rsum = rsum_ref[...]
    block = iota((128, 128), 0) // 8
    group = iota((128, 128), 1) // 32
    for j in range(4):
        rows = [
            jnp.concatenate([delta[4 * j + s][:, 32 * q : 32 * q + 32] for s in range(4)], axis=1)
            for q in range(4)
        ]
        ret = jnp.concatenate([last[4 * j + s : 4 * j + s + 1, 0:32] for s in range(4)], axis=1)
        rows.append(jnp.broadcast_to(ret, (8, 128)))
        spread = jnp.concatenate(rows, axis=0)
        cells = jnp.where(block == 4 * j + group, own, 0.0)
        weight = jnp.sum(cells, axis=0, keepdims=True)
        gram = gram + dot_t(spread * weight, spread)
        rsum = rsum + dot_t(spread, cells)
    pay_ref[128:256, :] = cross_ref[...]
    pay_ref[0:64, :] = rsum[0:64]
    ret = rsum[64:72]
    row = iota((8, 128), 0)
    extra = jnp.where(
        row == 0,
        pltpu.roll(ret, 65, 1),
        jnp.where(row == 1, pltpu.roll(ret, 2, 1), jnp.where(row == 2, pltpu.roll(ret, 67, 1), 0.0)),
    )
    wide = jnp.concatenate([gram[0:64], jnp.zeros((64, 128 - ROWS), F32)], axis=1)
    extra = jnp.concatenate([extra, jnp.zeros((56, 128), F32)], axis=0)
    pay_ref[64:128, :] = jnp.where(iota((64, 128), 1) < 65, wide, extra)


def eliminate(a):
    rowid = iota((64, 128), 0)
    for k in range(0, K, 4):
        cols = [jnp.broadcast_to(a[:, k + j : k + j + 1], (64, 128)) for j in range(4)]
        rows = [a[k + i : k + i + 1, :] for i in range(4)]
        block = [[cols[j][k + i : k + i + 1, :] for j in range(4)] for i in range(4)]
        for i in range(4):
            inverse = 1.0 / block[i][i]
            rows[i] = rows[i] * inverse
            for j in range(i + 1, 4):
                block[i][j] = block[i][j] * inverse
            for m in range(4):
                if m != i:
                    rows[m] = rows[m] - block[m][i] * rows[i]
                    for j in range(i + 1, 4):
                        block[m][j] = block[m][j] - block[m][i] * block[i][j]
        rest = a
        for i in range(4):
            rest = rest - cols[i] * rows[i]
        for i in range(4):
            rest = jnp.where(rowid == k + i, rows[i], rest)
        a = rest
    return a


def solve_kernel(
    day_ref, side_ref, panel_hbm, pay_ref, near_ref, far_ref, mask_ref, count_ref, coef_ref,
    out_ref, panel_ref, w_ref, sem,
):
    copy = pltpu.make_async_copy(panel_hbm, panel_ref, sem)
    copy.start()
    day = day_ref[0]
    lane = iota((1, 128), 1)
    head = pay_ref[64:72, :]
    ret = jnp.where(
        lane < 63,
        pltpu.roll(head, 63, 1)[0:1],
        jnp.where(lane < 126, pltpu.roll(head, 126, 1)[1:2], pltpu.roll(head, 61, 1)[2:3]),
    )
    r = jnp.concatenate([pay_ref[0:64, :], jnp.broadcast_to(ret, (8, 128))], axis=0)
    cross = pay_ref[128:256, :]
    n = count_ref[1:2, 0:128]
    d1 = r / n
    q1 = dot(d1, cross)
    d2 = q1 / n
    q2 = dot(d2, cross)
    d3 = q2 / n
    right = jnp.concatenate([d1 + d2, d2 + d3, d3], axis=1)
    right = jnp.concatenate([right, jnp.zeros((128 - ROWS, 384), F32)], axis=0)
    left = jnp.concatenate([r[0:64], q1[0:64], q2[0:64]], axis=1)
    solved = eliminate(pay_ref[64:128, :] - dot_t(left, right))
    coef = jnp.broadcast_to(solved[:, 64:65], (64, 128))
    picked = jnp.where(iota((64, 128), 0) == iota((64, 128), 1), coef, 0.0)
    coef_ref[...] = jnp.sum(picked, axis=0, keepdims=True)[:, 0:K]
    w = jnp.concatenate([-coef, (iota((8, 128), 0) == 0).astype(F32)], axis=0)
    w_ref[...] = w
    e = d1 + d2
    ew = jnp.sum(w * e, axis=0, keepdims=True)
    dw = jnp.sum(w * (e + d3), axis=0, keepdims=True)
    back = dot(jnp.broadcast_to(ew, (8, 128)), mask_ref[...])[0:1]
    here = iota((8, 128), 1) == 8 * day + iota((8, 128), 0)
    dw = jnp.sum(jnp.where(here, dw, 0.0), axis=1, keepdims=True)
    packed = jnp.zeros((16, 128), F32)
    for q in range(4):
        packed = jnp.where(iota((16, 128), 1) // 32 == q, w[16 * q : 16 * q + 16], packed)
    core = day % 2
    first = 25 * 8 * side_ref[0]

    def part(ref, z):
        row = first + 25 * z + 8
        one = jnp.sum(packed * ref[pl.ds(row, 16), :], axis=0, keepdims=True)
        return one + jnp.where(lane < 32, ref[pl.ds(row + 16, 1), :], 0.0)

    parts = []
    for z in range(8):
        mine, theirs = part(near_ref, z), part(far_ref, z)
        parts += [jnp.where(core == 0, mine, theirs), jnp.where(core == 0, theirs, mine)]
    parts = jnp.concatenate(parts, axis=0)
    parts = parts + pltpu.roll(parts, 32, 1)
    parts = parts + pltpu.roll(parts, 64, 1)
    parts = jnp.where(iota((16, 128), 1) // 32 == iota((16, 128), 0) % 4, parts, 0.0)
    firm = jnp.concatenate(
        [jnp.sum(parts[4 * j : 4 * j + 4], axis=0, keepdims=True) for j in range(4)], axis=1
    )
    firm = back / count_ref[0:1, :] - firm
    mask = mask_ref[pl.ds(pl.multiple_of(day * 8, 8), 8), :]
    copy.wait()
    acc = panel_ref[32 * K : 32 * K + 32, :]
    for c in range(K):
        weight = jnp.broadcast_to(w_ref[c : c + 1, :], (32, 128))
        acc = acc + weight * panel_ref[32 * c : 32 * c + 32, :]
    acc = jnp.concatenate([acc[8 * j : 8 * j + 8] for j in range(4)], axis=1)
    out_ref[...] = mask * (acc + firm - dw)


def call(kernel, out, spaces, scratch, *args):
    kinds = {"s": pltpu.SMEM, "v": pltpu.VMEM, "p": pltpu.VMEM, "h": pl.ANY}
    args = [
        pltpu.with_memory_space_constraint(a, pltpu.VMEM) if s == "v" else a
        for s, a in zip(spaces, args)
    ]
    return pl.pallas_call(
        kernel,
        out_shape=[pltpu.VMEM(s, F32) if v else jax.ShapeDtypeStruct(s, F32) for s, v in out],
        in_specs=[pl.BlockSpec(memory_space=kinds[s]) for s in spaces],
        out_specs=[pl.BlockSpec(memory_space=pltpu.VMEM) for _ in out],
        scratch_shapes=scratch,
        name=kernel.__name__,
    )(*args)


PANEL = pltpu.VMEM((65 * 32, 128), F32)


def sums(day, panel, presence):
    scratch = [PANEL, pltpu.VMEM((8, 512), jnp.int32), pltpu.SemaphoreType.DMA((6,))]
    return call(sums_kernel, [((272, 128), True)], "shh", scratch, day, panel, presence)[0]


def scatter(day, panel, presence, day_n):
    shapes = [((n, 128), True) for n in (ROWS, ROWS, 128, 128)]
    shapes += [((128, 512), True), ((8, 512), True)]
    return call(scatter_kernel, shapes, "sppp", [], day, panel, presence, day_n)


def owner(*args):
    return call(owner_kernel, [((256, 128), True), ((17, 128), True)], "vvvvv", [], *args)


def solve(*args):
    scratch = [PANEL, pltpu.VMEM((ROWS, 128), F32), pltpu.SemaphoreType.DMA]
    return call(
        solve_kernel, [((1, K), False), ((8, 512), False)], "sshvvvvv", scratch, *args
    )


def exchange(x, axes):
    return lax.all_to_all(x, axes, 0, 0, tiled=True)


def on_device(panel, presence, firm_count, day_count):
    day = lax.axis_index(("z", "c")).astype(jnp.int32).reshape(1)
    side = lax.axis_index("h").astype(jnp.int32).reshape(1)
    panel = panel.reshape(65, 8, 4, 128).transpose(0, 2, 1, 3).reshape(65 * 32, 128)
    msg = exchange(sums(day, panel, presence).reshape(16, 1, 17 * 128), ("z", "c"))
    *here, mask, count = scatter(day, panel, presence, day_count.reshape(1, 128))
    pay, mean = owner(msg.reshape(272, 128), *here)
    pay = jnp.sum(exchange(pay.reshape(32, 8, 128), ("x", "y", "c")), axis=0)
    near = jnp.concatenate([pay.reshape(1, 1, 8 * 128), mean.reshape(1, 1, 17 * 128)], axis=2)
    near = exchange(jnp.broadcast_to(near, (16, 1, 25 * 128)), ("h", "z"))
    far = lax.ppermute(near, "c", ((0, 1), (1, 0)))
    pay = jnp.sum(near[:, 0, : 8 * 128], axis=0).reshape(8, 128)
    pay = exchange(jnp.broadcast_to(pay[None], (32, 8, 128)), ("x", "y", "c")).reshape(256, 128)
    near, far = near.reshape(400, 128), far.reshape(400, 128)
    coef, residual = solve(day, side, panel, pay, near, far, mask, count)
    return coef.reshape(K), residual


def solution(mesh):
    split = Mesh(mesh.devices.reshape(4, 4, 2, 8, 2), ("x", "y", "h", "z", "c"))
    firm, day = ("x", "y", "h"), ("z", "c")
    return jax.shard_map(
        on_device,
        mesh=split,
        in_specs=(P(None, day, firm), P(None, firm), P(firm), P()),
        out_specs=(P(), P(day, firm)),
        check_vma=False,
    )
```

```python
import jax
import jax.numpy as jnp
from jax import lax
from jax.experimental import pallas as pl
from jax.experimental.pallas import tpu as pltpu
from jax.sharding import Mesh, PartitionSpec as P


K = 64
ROWS = 72
HIGHEST = lax.Precision.HIGHEST
F32 = jnp.float32


def iota(shape, axis):
    return lax.broadcasted_iota(jnp.int32, shape, axis)


def dot_t(a, b):
    return lax.dot_general(
        a, b, (((1,), (1,)), ((), ())), precision=HIGHEST, preferred_element_type=F32
    )


def dot(a, b):
    return lax.dot_general(
        a, b, (((1,), (0,)), ((), ())), precision=HIGHEST, preferred_element_type=F32
    )


def stacked(panel_ref, t):
    tiles = []
    for j in range(4):
        row = 8 * j + t
        target = panel_ref[32 * K + row : 32 * K + row + 1, :]
        regress = panel_ref[pl.ds(row, K, stride=32), :]
        tiles.append(jnp.concatenate([regress, jnp.broadcast_to(target, (8, 128))], axis=0))
    return jnp.concatenate(tiles, axis=1)


def sums_kernel(day_ref, panel_hbm, pres_hbm, msg_ref, panel_ref, pres_ref, sems):
    start = pl.multiple_of(day_ref[0] * 8, 8)
    copies = [pltpu.make_async_copy(pres_hbm.at[pl.ds(start, 8), :], pres_ref, sems.at[0])]
    pieces = [slice(512 * q, 512 * q + 512) for q in range(4)] + [slice(32 * K, 32 * K + 32)]
    for i, rows in enumerate(pieces):
        copies.append(
            pltpu.make_async_copy(panel_hbm.at[rows, :], panel_ref.at[rows, :], sems.at[i + 1])
        )
    for copy in copies:
        copy.start()
    copies[0].wait()
    mask = pres_ref[...].astype(F32)
    low = [iota((8, 128), 0) % (2 * n) < n for n in (4, 2, 1)]
    for q in range(4):
        copies[q + 1].wait()
        tiles = []
        for j in range(4):
            held = mask[:, 128 * j : 128 * j + 128]
            halves = []
            for half in range(2):
                base = 512 * q + 256 * half + 8 * j
                rows = [base + 32 * c for c in (0, 4, 2, 6, 1, 5, 3, 7)]
                level = [panel_ref[r : r + 8, :] * held for r in rows]
                for n, mine in zip((4, 2, 1), low):
                    level = [
                        jnp.where(mine, x + pltpu.roll(x, 8 - n, 0), y + pltpu.roll(y, n, 0))
                        for x, y in zip(level[0::2], level[1::2])
                    ]
                halves.append(level[0])
            tiles.append(jnp.concatenate(halves, axis=0))
        for d in range(16):
            lanes = slice(32 * (d % 4), 32 * (d % 4) + 32)
            msg_ref[17 * d : 17 * d + 16, 32 * q : 32 * q + 32] = tiles[d // 4][:, lanes]
    copies[5].wait()
    for j in range(4):
        x = panel_ref[32 * K + 8 * j : 32 * K + 8 * j + 8, :] * mask[:, 128 * j : 128 * j + 128]
        total = jnp.sum(x, axis=0, keepdims=True)
        for s in range(4):
            d = 4 * j + s
            msg_ref[17 * d + 16 : 17 * d + 17, :] = jnp.zeros((1, 128), F32)
            msg_ref[17 * d + 16 : 17 * d + 17, 0:32] = total[:, 32 * s : 32 * s + 32]


def scatter_kernel(
    day_ref, panel_ref, pres_ref, dayn_ref, gram_ref, rsum_ref, own_ref, cross_ref, mask_ref, count_ref
):
    day = day_ref[0]
    every = pres_ref[...].astype(F32)
    mask_ref[...] = every
    firm_n = jnp.sum(every, axis=0, keepdims=True)
    day_n = jnp.concatenate([dayn_ref[...].astype(F32), jnp.zeros((1, 384), F32)], axis=1)
    count_ref[...] = jnp.concatenate([firm_n, day_n, jnp.zeros((6, 512), F32)], axis=0)
    mask = mask_ref[pl.ds(pl.multiple_of(day * 8, 8), 8), :]
    count = jnp.sum(mask, axis=0, keepdims=True)
    total = mask[0:1] * stacked(panel_ref, 0)
    for t in range(1, 8):
        total = total + mask[t : t + 1] * stacked(panel_ref, t)
    mean = total / jnp.maximum(count, 1.0)
    gram = jnp.zeros((ROWS, ROWS), F32)
    rsum = jnp.zeros((ROWS, 128), F32)
    lane = iota((ROWS, 128), 1)
    for t in range(8):
        centred = mask[t : t + 1] * (stacked(panel_ref, t) - mean)
        gram = gram + dot_t(centred, centred)
        sums = jnp.sum(centred, axis=1, keepdims=True)
        rsum = rsum + jnp.where(lane == 8 * day + t, sums, 0.0)
    gram_ref[...] = jnp.concatenate([gram, jnp.zeros((ROWS, 128 - ROWS), F32)], axis=1)
    rsum_ref[...] = rsum
    pick = (iota((512, 128), 0) == 32 * day + iota((512, 128), 1) % 32).astype(jnp.bfloat16)
    own = lax.dot_general(
        every.astype(jnp.bfloat16), pick, (((1,), (0,)), ((), ())),
        preferred_element_type=F32,
    )
    own_ref[...] = own
    firm_n = jnp.sum(own, axis=0, keepdims=True)
    weight = jnp.where(iota((1, 128), 1) < 32, 1.0 / firm_n, 0.0)
    cross_ref[...] = dot_t(own * weight, own)


def owner_kernel(msg_ref, gram_ref, rsum_ref, own_ref, cross_ref, pay_ref, mean_ref):
    own = own_ref[...]
    per_block = jnp.sum(own.reshape(16, 8, 128), axis=1)
    firm_n = jnp.sum(per_block, axis=0, keepdims=True)
    msg = [msg_ref[17 * b : 17 * b + 16, :] for b in range(16)]
    last = jnp.concatenate([msg_ref[17 * b + 16 : 17 * b + 17, :] for b in range(16)], axis=0)
    total = msg[0]
    for b in range(1, 16):
        total = total + msg[b]
    mean = total / firm_n
    last_mean = jnp.sum(last, axis=0, keepdims=True) / firm_n
    for k in range(16):
        mean_ref[:, 128 * k : 128 * k + 128] = mean[k : k + 1]
    mean_ref[:, 2048:2176] = last_mean
    held = jnp.maximum(per_block, 1.0)
    delta = [msg[b] / held[b : b + 1] - mean for b in range(16)]
    last = last / held - last_mean

    gram = gram_ref[:, 0:ROWS]
    rsum = rsum_ref[...]
    block = iota((128, 128), 0) // 8
    group = iota((128, 128), 1) // 32
    for j in range(4):
        rows = [
            jnp.concatenate([delta[4 * j + s][:, 32 * q : 32 * q + 32] for s in range(4)], axis=1)
            for q in range(4)
        ]
        ret = jnp.concatenate([last[4 * j + s : 4 * j + s + 1, 0:32] for s in range(4)], axis=1)
        rows.append(jnp.broadcast_to(ret, (8, 128)))
        spread = jnp.concatenate(rows, axis=0)
        cells = jnp.where(block == 4 * j + group, own, 0.0)
        weight = jnp.sum(cells, axis=0, keepdims=True)
        gram = gram + dot_t(spread * weight, spread)
        rsum = rsum + dot_t(spread, cells)
    wide = jnp.concatenate([gram, jnp.zeros((ROWS, 128 - ROWS), F32)], axis=1)
    ret, rhs, row = rsum[64:72], wide[64:72], iota((8, 128), 0)
    extra = jnp.where(
        row == 0,
        ret,
        jnp.where(row == 1, pltpu.roll(ret, 96, 1), jnp.where(row == 2, rhs, pltpu.roll(rhs, 96, 1))),
    )
    extra = jnp.concatenate([extra, jnp.zeros((24, 128), F32)], axis=0)
    lane = iota((32, 128), 1)
    pay_ref[0:64, :] = rsum[0:64]
    pay_ref[64:128, :] = cross_ref[0:64, :]
    pay_ref[128:160, :] = jnp.where(lane < 64, wide[0:32], cross_ref[64:96, :])
    pay_ref[160:192, :] = jnp.where(
        lane // 32 == 1, wide[32:64], jnp.where(lane // 32 == 3, cross_ref[96:128, :], extra)
    )


def eliminate(a):
    rowid = iota((64, 128), 0)
    for k in range(0, K, 4):
        cols = [jnp.broadcast_to(a[:, k + j : k + j + 1], (64, 128)) for j in range(4)]
        rows = [a[k + i : k + i + 1, :] for i in range(4)]
        block = [[cols[j][k + i : k + i + 1, :] for j in range(4)] for i in range(4)]
        for i in range(4):
            inverse = 1.0 / block[i][i]
            rows[i] = rows[i] * inverse
            for j in range(i + 1, 4):
                block[i][j] = block[i][j] * inverse
            for m in range(4):
                if m != i:
                    rows[m] = rows[m] - block[m][i] * rows[i]
                    for j in range(i + 1, 4):
                        block[m][j] = block[m][j] - block[m][i] * block[i][j]
        rest = a
        for i in range(4):
            rest = rest - cols[i] * rows[i]
        for i in range(4):
            rest = jnp.where(rowid == k + i, rows[i], rest)
        a = rest
    return a


def solve_kernel(
    day_ref, side_ref, panel_hbm, pay_ref, near_ref, far_ref, mask_ref, count_ref, coef_ref,
    out_ref, panel_ref, w_ref, sem,
):
    copy = pltpu.make_async_copy(panel_hbm, panel_ref, sem)
    copy.start()
    day = day_ref[0]
    lane = iota((1, 128), 1)
    head = pay_ref[160:168, :]
    moved = pltpu.roll(head, 32, 1)
    ret = jnp.where(lane // 32 % 2 == 0, head[0:1], moved[1:2])
    rhs = jnp.where(lane < 32, head[2:3], moved[3:4])
    r = jnp.concatenate([pay_ref[0:64, :], jnp.broadcast_to(ret, (8, 128))], axis=0)
    top, mid, low = pay_ref[64:128, :], pay_ref[128:160, :], pay_ref[160:192, :]
    wide = iota((32, 128), 1)
    upper = [
        jnp.where(wide >= 64, top[0:32], jnp.where(wide >= 32, mid, 0.0)),
        jnp.where(wide >= 64, top[32:64], 0.0),
        jnp.where(
            wide >= 96, mid, jnp.where((iota((32, 128), 0) == 0) & (wide < 64), rhs, 0.0)
        ),
        jnp.zeros((32, 128), F32),
    ]
    lower = jnp.concatenate(upper, axis=0).T
    cross = jnp.concatenate(
        [
            top,
            jnp.where(wide >= 64, mid, 0.0) + lower[64:96],
            jnp.where(wide >= 96, low, 0.0) + lower[96:128],
        ],
        axis=0,
    )
    gram = jnp.concatenate(
        [
            jnp.where(wide < 64, mid, 0.0) + lower[0:32],
            jnp.where(wide // 32 == 1, low, 0.0) + lower[32:64],
        ],
        axis=0,
    )
    n = count_ref[1:2, 0:128]
    d1 = r / n
    q1 = dot(d1, cross)
    d2 = q1 / n
    q2 = dot(d2, cross)
    d3 = q2 / n
    right = jnp.concatenate([d1 + d2, d2 + d3, d3], axis=1)
    right = jnp.concatenate([right, jnp.zeros((128 - ROWS, 384), F32)], axis=0)
    left = jnp.concatenate([r[0:64], q1[0:64], q2[0:64]], axis=1)
    solved = eliminate(gram - dot_t(left, right))
    coef = jnp.broadcast_to(solved[:, 64:65], (64, 128))
    picked = jnp.where(iota((64, 128), 0) == iota((64, 128), 1), coef, 0.0)
    coef_ref[...] = jnp.sum(picked, axis=0, keepdims=True)[:, 0:K]
    w = jnp.concatenate([-coef, (iota((8, 128), 0) == 0).astype(F32)], axis=0)
    w_ref[...] = w
    e = d1 + d2
    ew = jnp.sum(w * e, axis=0, keepdims=True)
    dw = jnp.sum(w * (e + d3), axis=0, keepdims=True)
    back = dot(jnp.broadcast_to(ew, (8, 128)), mask_ref[...])[0:1]
    here = iota((8, 128), 1) == 8 * day + iota((8, 128), 0)
    dw = jnp.sum(jnp.where(here, dw, 0.0), axis=1, keepdims=True)
    packed = jnp.zeros((16, 128), F32)
    for q in range(4):
        packed = jnp.where(iota((16, 128), 1) // 32 == q, w[16 * q : 16 * q + 16], packed)
    core = day % 2
    first = 23 * 8 * side_ref[0]

    def part(ref, z):
        row = first + 23 * z + 6
        one = jnp.sum(packed * ref[pl.ds(row, 16), :], axis=0, keepdims=True)
        return one + jnp.where(lane < 32, ref[pl.ds(row + 16, 1), :], 0.0)

    parts = []
    for z in range(8):
        mine, theirs = part(near_ref, z), part(far_ref, z)
        parts += [jnp.where(core == 0, mine, theirs), jnp.where(core == 0, theirs, mine)]
    parts = jnp.concatenate(parts, axis=0)
    parts = parts + pltpu.roll(parts, 32, 1)
    parts = parts + pltpu.roll(parts, 64, 1)
    parts = jnp.where(iota((16, 128), 1) // 32 == iota((16, 128), 0) % 4, parts, 0.0)
    firm = jnp.concatenate(
        [jnp.sum(parts[4 * j : 4 * j + 4], axis=0, keepdims=True) for j in range(4)], axis=1
    )
    firm = back / count_ref[0:1, :] - firm
    mask = mask_ref[pl.ds(pl.multiple_of(day * 8, 8), 8), :]
    copy.wait()
    acc = panel_ref[32 * K : 32 * K + 32, :]
    for c in range(K):
        weight = jnp.broadcast_to(w_ref[c : c + 1, :], (32, 128))
        acc = acc + weight * panel_ref[32 * c : 32 * c + 32, :]
    acc = jnp.concatenate([acc[8 * j : 8 * j + 8] for j in range(4)], axis=1)
    out_ref[...] = mask * (acc + firm - dw)


def call(kernel, out, spaces, scratch, *args):
    kinds = {"s": pltpu.SMEM, "v": pltpu.VMEM, "p": pltpu.VMEM, "h": pl.ANY}
    args = [
        pltpu.with_memory_space_constraint(a, pltpu.VMEM) if s == "v" else a
        for s, a in zip(spaces, args)
    ]
    return pl.pallas_call(
        kernel,
        out_shape=[pltpu.VMEM(s, F32) if v else jax.ShapeDtypeStruct(s, F32) for s, v in out],
        in_specs=[pl.BlockSpec(memory_space=kinds[s]) for s in spaces],
        out_specs=[pl.BlockSpec(memory_space=pltpu.VMEM) for _ in out],
        scratch_shapes=scratch,
    )(*args)


PANEL = pltpu.VMEM((65 * 32, 128), F32)


def sums(day, panel, presence):
    scratch = [PANEL, pltpu.VMEM((8, 512), jnp.int32), pltpu.SemaphoreType.DMA((6,))]
    return call(sums_kernel, [((272, 128), True)], "shh", scratch, day, panel, presence)[0]


def scatter(day, panel, presence, day_n):
    shapes = [((n, 128), True) for n in (ROWS, ROWS, 128, 128)]
    shapes += [((128, 512), True), ((8, 512), True)]
    return call(scatter_kernel, shapes, "sppp", [], day, panel, presence, day_n)


def owner(*args):
    return call(owner_kernel, [((192, 128), True), ((1, 17 * 128), True)], "vvvvv", [], *args)


def solve(*args):
    scratch = [PANEL, pltpu.VMEM((ROWS, 128), F32), pltpu.SemaphoreType.DMA]
    return call(
        solve_kernel, [((1, K), False), ((8, 512), False)], "sshvvvvv", scratch, *args
    )


def exchange(x, axes):
    return lax.all_to_all(x, axes, 0, 0, tiled=True)


def on_device(panel, presence, firm_count, day_count):
    day = lax.axis_index(("z", "c")).astype(jnp.int32).reshape(1)
    side = lax.axis_index("h").astype(jnp.int32).reshape(1)
    panel = panel.reshape(65, 8, 4, 128).transpose(0, 2, 1, 3).reshape(65 * 32, 128)
    msg = exchange(sums(day, panel, presence).reshape(16, 1, 17 * 128), ("z", "c"))
    *here, mask, count = scatter(day, panel, presence, day_count.reshape(1, 128))
    pay, mean = owner(msg.reshape(272, 128), *here)
    pay = jnp.sum(exchange(pay.reshape(32, 1, 6 * 128), ("x", "y", "c")), axis=0)
    near = jnp.concatenate([pay, mean], axis=1).reshape(1, 1, 23 * 128)
    near = exchange(jnp.broadcast_to(near, (16, 1, 23 * 128)), ("h", "z"))
    pay = jnp.sum(near[:, :, : 6 * 128], axis=0)
    far = lax.ppermute(near, "c", ((0, 1), (1, 0)))
    pay = exchange(jnp.broadcast_to(pay[None], (32, 1, 6 * 128)), ("x", "y", "c"))
    pay = pay.reshape(192, 128)
    near, far = near.reshape(368, 128), far.reshape(368, 128)
    coef, residual = solve(day, side, panel, pay, near, far, mask, count)
    return coef.reshape(K), residual


def solution(mesh):
    split = Mesh(mesh.devices.reshape(4, 4, 2, 8, 2), ("x", "y", "h", "z", "c"))
    firm, day = ("x", "y", "h"), ("z", "c")
    return jax.shard_map(
        on_device,
        mesh=split,
        in_specs=(P(None, day, firm), P(None, firm), P(firm), P()),
        out_specs=(P(), P(day, firm)),
        check_vma=False,
    )
```

```python
import jax
import jax.numpy as jnp
from jax import lax
from jax.experimental import pallas as pl
from jax.experimental.pallas import tpu as pltpu
from jax.sharding import Mesh, PartitionSpec as P


K = 64
ROWS = 72
HIGHEST = lax.Precision.HIGHEST
F32 = jnp.float32


def iota(shape, axis):
    return lax.broadcasted_iota(jnp.int32, shape, axis)


def dot_t(a, b):
    return lax.dot_general(
        a, b, (((1,), (1,)), ((), ())), precision=HIGHEST, preferred_element_type=F32
    )


def dot(a, b):
    return lax.dot_general(
        a, b, (((1,), (0,)), ((), ())), precision=HIGHEST, preferred_element_type=F32
    )


def day_index():
    return lax.axis_index("z") * 2 + lax.axis_index("c")


def stacked(panel_ref, t):
    tiles = []
    for j in range(4):
        row = 8 * j + t
        target = panel_ref[32 * K + row : 32 * K + row + 1, :]
        regress = panel_ref[pl.ds(row, K, stride=32), :]
        tiles.append(jnp.concatenate([regress, jnp.broadcast_to(target, (8, 128))], axis=0))
    return jnp.concatenate(tiles, axis=1)


def sums_kernel(panel_hbm, pres_hbm, msg_ref, panel_ref, pres_ref, sems):
    start = pl.multiple_of(day_index() * 8, 8)
    copies = [pltpu.make_async_copy(pres_hbm.at[pl.ds(start, 8), :], pres_ref, sems.at[0])]
    pieces = [slice(512 * q, 512 * q + 512) for q in range(4)] + [slice(32 * K, 32 * K + 32)]
    for i, rows in enumerate(pieces):
        copies.append(
            pltpu.make_async_copy(panel_hbm.at[rows, :], panel_ref.at[rows, :], sems.at[i + 1])
        )
    for copy in copies:
        copy.start()
    copies[0].wait()
    mask = pres_ref[...].astype(F32)
    low = [iota((8, 128), 0) % (2 * n) < n for n in (4, 2, 1)]
    for q in range(4):
        copies[q + 1].wait()
        tiles = []
        for j in range(4):
            held = mask[:, 128 * j : 128 * j + 128]
            halves = []
            for half in range(2):
                base = 512 * q + 256 * half + 8 * j
                rows = [base + 32 * c for c in (0, 4, 2, 6, 1, 5, 3, 7)]
                level = [panel_ref[r : r + 8, :] * held for r in rows]
                for n, mine in zip((4, 2, 1), low):
                    level = [
                        jnp.where(mine, x + pltpu.roll(x, 8 - n, 0), y + pltpu.roll(y, n, 0))
                        for x, y in zip(level[0::2], level[1::2])
                    ]
                halves.append(level[0])
            tiles.append(jnp.concatenate(halves, axis=0))
        for d in range(16):
            lanes = slice(32 * (d % 4), 32 * (d % 4) + 32)
            msg_ref[17 * d : 17 * d + 16, 32 * q : 32 * q + 32] = tiles[d // 4][:, lanes]
    copies[5].wait()
    for j in range(4):
        x = panel_ref[32 * K + 8 * j : 32 * K + 8 * j + 8, :] * mask[:, 128 * j : 128 * j + 128]
        total = jnp.sum(x, axis=0, keepdims=True)
        for s in range(4):
            d = 4 * j + s
            msg_ref[17 * d + 16 : 17 * d + 17, :] = jnp.zeros((1, 128), F32)
            msg_ref[17 * d + 16 : 17 * d + 17, 0:32] = total[:, 32 * s : 32 * s + 32]


def scatter_kernel(
    panel_ref, pres_ref, dayn_ref, gram_ref, rsum_ref, own_ref, cross_ref, mask_ref, count_ref
):
    day = day_index()
    every = pres_ref[...].astype(F32)
    mask_ref[...] = every
    firm_n = jnp.sum(every, axis=0, keepdims=True)
    day_n = jnp.concatenate([dayn_ref[...].astype(F32), jnp.zeros((1, 384), F32)], axis=1)
    count_ref[...] = jnp.concatenate([firm_n, day_n, jnp.zeros((6, 512), F32)], axis=0)
    mask = mask_ref[pl.ds(pl.multiple_of(day * 8, 8), 8), :]
    count = jnp.sum(mask, axis=0, keepdims=True)
    total = mask[0:1] * stacked(panel_ref, 0)
    for t in range(1, 8):
        total = total + mask[t : t + 1] * stacked(panel_ref, t)
    mean = total / jnp.maximum(count, 1.0)
    gram = jnp.zeros((ROWS, ROWS), F32)
    rsum = jnp.zeros((ROWS, 128), F32)
    lane = iota((ROWS, 128), 1)
    for t in range(8):
        centred = mask[t : t + 1] * (stacked(panel_ref, t) - mean)
        gram = gram + dot_t(centred, centred)
        sums = jnp.sum(centred, axis=1, keepdims=True)
        rsum = rsum + jnp.where(lane == 8 * day + t, sums, 0.0)
    gram_ref[...] = jnp.concatenate([gram, jnp.zeros((ROWS, 128 - ROWS), F32)], axis=1)
    rsum_ref[...] = rsum
    pick = (iota((512, 128), 0) == 32 * day + iota((512, 128), 1) % 32).astype(jnp.bfloat16)
    own = lax.dot_general(
        every.astype(jnp.bfloat16), pick, (((1,), (0,)), ((), ())),
        preferred_element_type=F32,
    )
    own_ref[...] = own
    firm_n = jnp.sum(own, axis=0, keepdims=True)
    weight = jnp.where(iota((1, 128), 1) < 32, 1.0 / firm_n, 0.0)
    cross_ref[...] = dot_t(own * weight, own)


def owner_kernel(msg_ref, gram_ref, rsum_ref, own_ref, cross_ref, pay_ref, mean_ref):
    own = own_ref[...]
    per_block = jnp.sum(own.reshape(16, 8, 128), axis=1)
    firm_n = jnp.sum(per_block, axis=0, keepdims=True)
    msg = [msg_ref[17 * b : 17 * b + 16, :] for b in range(16)]
    last = jnp.concatenate([msg_ref[17 * b + 16 : 17 * b + 17, :] for b in range(16)], axis=0)
    total = msg[0]
    for b in range(1, 16):
        total = total + msg[b]
    mean = total / firm_n
    last_mean = jnp.sum(last, axis=0, keepdims=True) / firm_n
    for k in range(16):
        mean_ref[:, 128 * k : 128 * k + 128] = mean[k : k + 1]
    mean_ref[:, 2048:2176] = last_mean
    held = jnp.maximum(per_block, 1.0)
    delta = [msg[b] / held[b : b + 1] - mean for b in range(16)]
    last = last / held - last_mean

    gram = gram_ref[:, 0:ROWS]
    rsum = rsum_ref[...]
    block = iota((128, 128), 0) // 8
    group = iota((128, 128), 1) // 32
    for j in range(4):
        rows = [
            jnp.concatenate([delta[4 * j + s][:, 32 * q : 32 * q + 32] for s in range(4)], axis=1)
            for q in range(4)
        ]
        ret = jnp.concatenate([last[4 * j + s : 4 * j + s + 1, 0:32] for s in range(4)], axis=1)
        rows.append(jnp.broadcast_to(ret, (8, 128)))
        spread = jnp.concatenate(rows, axis=0)
        cells = jnp.where(block == 4 * j + group, own, 0.0)
        weight = jnp.sum(cells, axis=0, keepdims=True)
        gram = gram + dot_t(spread * weight, spread)
        rsum = rsum + dot_t(spread, cells)
    wide = jnp.concatenate([gram, jnp.zeros((ROWS, 128 - ROWS), F32)], axis=1)
    ret, rhs, row = rsum[64:72], wide[64:72], iota((8, 128), 0)
    extra = jnp.where(
        row == 0,
        ret,
        jnp.where(row == 1, pltpu.roll(ret, 96, 1), jnp.where(row == 2, rhs, pltpu.roll(rhs, 96, 1))),
    )
    extra = jnp.concatenate([extra, jnp.zeros((24, 128), F32)], axis=0)
    lane = iota((32, 128), 1)
    pay_ref[0:64, :] = rsum[0:64]
    pay_ref[64:128, :] = cross_ref[0:64, :]
    pay_ref[128:160, :] = jnp.where(lane < 64, wide[0:32], cross_ref[64:96, :])
    pay_ref[160:192, :] = jnp.where(
        lane // 32 == 1, wide[32:64], jnp.where(lane // 32 == 3, cross_ref[96:128, :], extra)
    )


def eliminate(a):
    rowid = iota((64, 128), 0)
    for k in range(0, K, 4):
        cols = [jnp.broadcast_to(a[:, k + j : k + j + 1], (64, 128)) for j in range(4)]
        rows = [a[k + i : k + i + 1, :] for i in range(4)]
        block = [[cols[j][k + i : k + i + 1, :] for j in range(4)] for i in range(4)]
        for i in range(4):
            inverse = 1.0 / block[i][i]
            rows[i] = rows[i] * inverse
            for j in range(i + 1, 4):
                block[i][j] = block[i][j] * inverse
            for m in range(4):
                if m != i:
                    rows[m] = rows[m] - block[m][i] * rows[i]
                    for j in range(i + 1, 4):
                        block[m][j] = block[m][j] - block[m][i] * block[i][j]
        rest = a
        for i in range(4):
            rest = rest - cols[i] * rows[i]
        for i in range(4):
            rest = jnp.where(rowid == k + i, rows[i], rest)
        a = rest
    return a


def solve_kernel(
    panel_hbm, pay_ref, near_ref, far_ref, mask_ref, count_ref, coef_ref,
    out_ref, panel_ref, w_ref, sem,
):
    copy = pltpu.make_async_copy(panel_hbm, panel_ref, sem)
    copy.start()
    day = day_index()
    lane = iota((1, 128), 1)
    head = pay_ref[160:168, :]
    moved = pltpu.roll(head, 32, 1)
    ret = jnp.where(lane // 32 % 2 == 0, head[0:1], moved[1:2])
    rhs = jnp.where(lane < 32, head[2:3], moved[3:4])
    r = jnp.concatenate([pay_ref[0:64, :], jnp.broadcast_to(ret, (8, 128))], axis=0)
    top, mid, low = pay_ref[64:128, :], pay_ref[128:160, :], pay_ref[160:192, :]
    wide = iota((32, 128), 1)
    upper = [
        jnp.where(wide >= 64, top[0:32], jnp.where(wide >= 32, mid, 0.0)),
        jnp.where(wide >= 64, top[32:64], 0.0),
        jnp.where(
            wide >= 96, mid, jnp.where((iota((32, 128), 0) == 0) & (wide < 64), rhs, 0.0)
        ),
        jnp.zeros((32, 128), F32),
    ]
    lower = jnp.concatenate(upper, axis=0).T
    cross = jnp.concatenate(
        [
            top,
            jnp.where(wide >= 64, mid, 0.0) + lower[64:96],
            jnp.where(wide >= 96, low, 0.0) + lower[96:128],
        ],
        axis=0,
    )
    gram = jnp.concatenate(
        [
            jnp.where(wide < 64, mid, 0.0) + lower[0:32],
            jnp.where(wide // 32 == 1, low, 0.0) + lower[32:64],
        ],
        axis=0,
    )
    n = count_ref[1:2, 0:128]
    d1 = r / n
    q1 = dot(d1, cross)
    d2 = q1 / n
    q2 = dot(d2, cross)
    d3 = q2 / n
    right = jnp.concatenate([d1 + d2, d2 + d3, d3], axis=1)
    right = jnp.concatenate([right, jnp.zeros((128 - ROWS, 384), F32)], axis=0)
    left = jnp.concatenate([r[0:64], q1[0:64], q2[0:64]], axis=1)
    solved = eliminate(gram - dot_t(left, right))
    coef = jnp.broadcast_to(solved[:, 64:65], (64, 128))
    picked = jnp.where(iota((64, 128), 0) == iota((64, 128), 1), coef, 0.0)
    coef_ref[...] = jnp.sum(picked, axis=0, keepdims=True)[:, 0:K]
    w = jnp.concatenate([-coef, (iota((8, 128), 0) == 0).astype(F32)], axis=0)
    w_ref[...] = w
    e = d1 + d2
    ew = jnp.sum(w * e, axis=0, keepdims=True)
    dw = jnp.sum(w * (e + d3), axis=0, keepdims=True)
    back = dot(jnp.broadcast_to(ew, (8, 128)), mask_ref[...])[0:1]
    here = iota((8, 128), 1) == 8 * day + iota((8, 128), 0)
    dw = jnp.sum(jnp.where(here, dw, 0.0), axis=1, keepdims=True)
    packed = jnp.zeros((16, 128), F32)
    for q in range(4):
        packed = jnp.where(iota((16, 128), 1) // 32 == q, w[16 * q : 16 * q + 16], packed)
    core = day % 2
    first = 23 * 8 * lax.axis_index("h")

    def part(ref, z):
        row = first + 23 * z + 6
        one = jnp.sum(packed * ref[pl.ds(row, 16), :], axis=0, keepdims=True)
        return one + jnp.where(lane < 32, ref[pl.ds(row + 16, 1), :], 0.0)

    parts = []
    for z in range(8):
        mine, theirs = part(near_ref, z), part(far_ref, z)
        parts += [jnp.where(core == 0, mine, theirs), jnp.where(core == 0, theirs, mine)]
    parts = jnp.concatenate(parts, axis=0)
    parts = parts + pltpu.roll(parts, 32, 1)
    parts = parts + pltpu.roll(parts, 64, 1)
    parts = jnp.where(iota((16, 128), 1) // 32 == iota((16, 128), 0) % 4, parts, 0.0)
    firm = jnp.concatenate(
        [jnp.sum(parts[4 * j : 4 * j + 4], axis=0, keepdims=True) for j in range(4)], axis=1
    )
    firm = back / count_ref[0:1, :] - firm
    mask = mask_ref[pl.ds(pl.multiple_of(day * 8, 8), 8), :]
    copy.wait()
    acc = panel_ref[32 * K : 32 * K + 32, :]
    for c in range(K):
        weight = jnp.broadcast_to(w_ref[c : c + 1, :], (32, 128))
        acc = acc + weight * panel_ref[32 * c : 32 * c + 32, :]
    acc = jnp.concatenate([acc[8 * j : 8 * j + 8] for j in range(4)], axis=1)
    out_ref[...] = mask * (acc + firm - dw)


def call(kernel, out, spaces, scratch, *args):
    kinds = {"v": pltpu.VMEM, "p": pltpu.VMEM, "h": pl.ANY}
    args = [
        pltpu.with_memory_space_constraint(a, pltpu.VMEM) if s == "v" else a
        for s, a in zip(spaces, args)
    ]
    return pl.pallas_call(
        kernel,
        out_shape=[pltpu.VMEM(s, F32) if v else jax.ShapeDtypeStruct(s, F32) for s, v in out],
        in_specs=[pl.BlockSpec(memory_space=kinds[s]) for s in spaces],
        out_specs=[pl.BlockSpec(memory_space=pltpu.VMEM) for _ in out],
        scratch_shapes=scratch,
    )(*args)


PANEL = pltpu.VMEM((65 * 32, 128), F32)


def sums(panel, presence):
    scratch = [PANEL, pltpu.VMEM((8, 512), jnp.int32), pltpu.SemaphoreType.DMA((6,))]
    return call(sums_kernel, [((272, 128), True)], "hh", scratch, panel, presence)[0]


def scatter(panel, presence, day_n):
    shapes = [((n, 128), True) for n in (ROWS, ROWS, 128, 128)]
    shapes += [((128, 512), True), ((8, 512), True)]
    return call(scatter_kernel, shapes, "ppp", [], panel, presence, day_n)


def owner(*args):
    return call(owner_kernel, [((192, 128), True), ((1, 17 * 128), True)], "vvvvv", [], *args)


def solve(*args):
    scratch = [PANEL, pltpu.VMEM((ROWS, 128), F32), pltpu.SemaphoreType.DMA]
    return call(
        solve_kernel, [((1, K), False), ((8, 512), False)], "hvvvvv", scratch, *args
    )


def exchange(x, axes):
    return lax.all_to_all(x, axes, 0, 0, tiled=True)


def on_device(panel, presence, firm_count, day_count):
    panel = panel.reshape(65, 8, 4, 128).transpose(0, 2, 1, 3).reshape(65 * 32, 128)
    msg = exchange(sums(panel, presence).reshape(16, 1, 17 * 128), ("z", "c"))
    *here, mask, count = scatter(panel, presence, day_count.reshape(1, 128))
    pay, mean = owner(msg.reshape(272, 128), *here)
    pay = jnp.sum(exchange(pay.reshape(32, 1, 6 * 128), ("x", "y", "c")), axis=0)
    near = jnp.concatenate([pay, mean], axis=1).reshape(1, 1, 23 * 128)
    near = exchange(jnp.broadcast_to(near, (16, 1, 23 * 128)), ("h", "z"))
    pay = jnp.sum(near[:, :, : 6 * 128], axis=0)
    far = lax.ppermute(near, "c", ((0, 1), (1, 0)))
    pay = exchange(jnp.broadcast_to(pay[None], (32, 1, 6 * 128)), ("x", "y", "c"))
    pay = pay.reshape(192, 128)
    near, far = near.reshape(368, 128), far.reshape(368, 128)
    coef, residual = solve(panel, pay, near, far, mask, count)
    return coef.reshape(K), residual


def solution(mesh):
    split = Mesh(mesh.devices.reshape(4, 4, 2, 8, 2), ("x", "y", "h", "z", "c"))
    firm, day = ("x", "y", "h"), ("z", "c")
    return jax.shard_map(
        on_device,
        mesh=split,
        in_specs=(P(None, day, firm), P(None, firm), P(firm), P()),
        out_specs=(P(), P(day, firm)),
        check_vma=False,
    )
```

```python
import jax
import jax.numpy as jnp
from jax import lax
from jax.experimental import pallas as pl
from jax.experimental.pallas import tpu as pltpu
from jax.sharding import Mesh, PartitionSpec as P


K = 64
ROWS = 72
HIGHEST = lax.Precision.HIGHEST
F32 = jnp.float32


def iota(shape, axis):
    return lax.broadcasted_iota(jnp.int32, shape, axis)


def dot_t(a, b):
    return lax.dot_general(
        a, b, (((1,), (1,)), ((), ())), precision=HIGHEST, preferred_element_type=F32
    )


def thirds(a):
    high = a.astype(jnp.bfloat16).astype(F32)
    rest = a - high
    mid = rest.astype(jnp.bfloat16).astype(F32)
    return [high, mid, rest - mid]


def dot(a, b):
    return lax.dot_general(
        a, b, (((1,), (0,)), ((), ())), precision=HIGHEST, preferred_element_type=F32
    )


def stacked(panel_ref, t):
    tiles = []
    for j in range(4):
        row = 8 * j + t
        target = panel_ref[32 * K + row : 32 * K + row + 1, :]
        regress = panel_ref[pl.ds(row, K, stride=32), :]
        tiles.append(jnp.concatenate([regress, jnp.broadcast_to(target, (8, 128))], axis=0))
    return jnp.concatenate(tiles, axis=1)


def sums_kernel(day_ref, panel_hbm, pres_hbm, msg_ref, panel_ref, pres_ref, sems):
    start = pl.multiple_of(day_ref[0] * 8, 8)
    copies = [pltpu.make_async_copy(pres_hbm.at[pl.ds(start, 8), :], pres_ref, sems.at[0])]
    pieces = [slice(512 * q, 512 * q + 512) for q in range(4)] + [slice(32 * K, 32 * K + 32)]
    for i, rows in enumerate(pieces):
        copies.append(
            pltpu.make_async_copy(panel_hbm.at[rows, :], panel_ref.at[rows, :], sems.at[i + 1])
        )
    for copy in copies:
        copy.start()
    copies[0].wait()
    mask = pres_ref[...].astype(F32)
    low = [iota((8, 128), 0) % (2 * n) < n for n in (4, 2, 1)]
    for q in range(4):
        copies[q + 1].wait()
        tiles = []
        for j in range(4):
            held = mask[:, 128 * j : 128 * j + 128]
            halves = []
            for half in range(2):
                base = 512 * q + 256 * half + 8 * j
                rows = [base + 32 * c for c in (0, 4, 2, 6, 1, 5, 3, 7)]
                level = [panel_ref[r : r + 8, :] * held for r in rows]
                for n, mine in zip((4, 2, 1), low):
                    level = [
                        jnp.where(mine, x + pltpu.roll(x, 8 - n, 0), y + pltpu.roll(y, n, 0))
                        for x, y in zip(level[0::2], level[1::2])
                    ]
                halves.append(level[0])
            tiles.append(jnp.concatenate(halves, axis=0))
        for d in range(16):
            lanes = slice(32 * (d % 4), 32 * (d % 4) + 32)
            msg_ref[17 * d : 17 * d + 16, 32 * q : 32 * q + 32] = tiles[d // 4][:, lanes]
    copies[5].wait()
    for j in range(4):
        x = panel_ref[32 * K + 8 * j : 32 * K + 8 * j + 8, :] * mask[:, 128 * j : 128 * j + 128]
        total = jnp.sum(x, axis=0, keepdims=True)
        for s in range(4):
            d = 4 * j + s
            msg_ref[17 * d + 16 : 17 * d + 17, :] = jnp.zeros((1, 128), F32)
            msg_ref[17 * d + 16 : 17 * d + 17, 0:32] = total[:, 32 * s : 32 * s + 32]


def scatter_kernel(
    day_ref, panel_ref, pres_ref, dayn_ref, gram_ref, rsum_ref, own_ref, cross_ref, mask_ref, count_ref
):
    day = day_ref[0]
    every = pres_ref[...].astype(F32)
    mask_ref[...] = every
    firm_n = jnp.sum(every, axis=0, keepdims=True)
    day_n = jnp.concatenate([dayn_ref[...].astype(F32), jnp.zeros((1, 384), F32)], axis=1)
    count_ref[...] = jnp.concatenate([firm_n, day_n, jnp.zeros((6, 512), F32)], axis=0)
    mask = mask_ref[pl.ds(pl.multiple_of(day * 8, 8), 8), :]
    count = jnp.sum(mask, axis=0, keepdims=True)
    total = mask[0:1] * stacked(panel_ref, 0)
    for t in range(1, 8):
        total = total + mask[t : t + 1] * stacked(panel_ref, t)
    mean = total / jnp.maximum(count, 1.0)
    gram = jnp.zeros((ROWS, ROWS), F32)
    rsum = jnp.zeros((ROWS, 128), F32)
    lane = iota((ROWS, 128), 1)
    for t in range(8):
        centred = mask[t : t + 1] * (stacked(panel_ref, t) - mean)
        gram = gram + dot_t(centred, centred)
        sums = jnp.sum(centred, axis=1, keepdims=True)
        rsum = rsum + jnp.where(lane == 8 * day + t, sums, 0.0)
    gram_ref[...] = jnp.concatenate([gram, jnp.zeros((ROWS, 128 - ROWS), F32)], axis=1)
    rsum_ref[...] = rsum
    pick = (iota((512, 128), 0) == 32 * day + iota((512, 128), 1) % 32).astype(jnp.bfloat16)
    own = lax.dot_general(
        every.astype(jnp.bfloat16), pick, (((1,), (0,)), ((), ())),
        preferred_element_type=F32,
    )
    own_ref[...] = own
    firm_n = jnp.sum(own, axis=0, keepdims=True)
    weight = jnp.where(iota((1, 128), 1) < 32, 1.0 / firm_n, 0.0)
    cross_ref[...] = dot_t(own * weight, own)


def owner_kernel(msg_ref, gram_ref, rsum_ref, own_ref, cross_ref, pay_ref, mean_ref):
    own = own_ref[...]
    per_block = jnp.sum(own.reshape(16, 8, 128), axis=1)
    firm_n = jnp.sum(per_block, axis=0, keepdims=True)
    msg = [msg_ref[17 * b : 17 * b + 16, :] for b in range(16)]
    last = jnp.concatenate([msg_ref[17 * b + 16 : 17 * b + 17, :] for b in range(16)], axis=0)
    total = msg[0]
    for b in range(1, 16):
        total = total + msg[b]
    mean = total / firm_n
    last_mean = jnp.sum(last, axis=0, keepdims=True) / firm_n
    for k in range(16):
        mean_ref[:, 128 * k : 128 * k + 128] = mean[k : k + 1]
    mean_ref[:, 2048:2176] = last_mean
    held = jnp.maximum(per_block, 1.0)
    delta = [msg[b] / held[b : b + 1] - mean for b in range(16)]
    last = last / held - last_mean

    gram = gram_ref[:, 0:ROWS]
    rsum = rsum_ref[...]
    block = iota((128, 128), 0) // 8
    group = iota((128, 128), 1) // 32
    for j in range(4):
        rows = [
            jnp.concatenate([delta[4 * j + s][:, 32 * q : 32 * q + 32] for s in range(4)], axis=1)
            for q in range(4)
        ]
        ret = jnp.concatenate([last[4 * j + s : 4 * j + s + 1, 0:32] for s in range(4)], axis=1)
        rows.append(jnp.broadcast_to(ret, (8, 128)))
        spread = jnp.concatenate(rows, axis=0)
        cells = jnp.where(block == 4 * j + group, own, 0.0)
        weight = jnp.sum(cells, axis=0, keepdims=True)
        gram = gram + dot_t(spread * weight, spread)
        three = jnp.concatenate(thirds(spread) + [jnp.zeros((8, 128), F32)], axis=0)
        sums = lax.dot_general(
            three.astype(jnp.bfloat16), cells.astype(jnp.bfloat16), (((1,), (1,)), ((), ())),
            preferred_element_type=F32,
        )
        rsum = rsum + (sums[0:72] + sums[72:144] + sums[144:216])
    wide = jnp.concatenate([gram, jnp.zeros((ROWS, 128 - ROWS), F32)], axis=1)
    ret, rhs, row = rsum[64:72], wide[64:72], iota((8, 128), 0)
    extra = jnp.where(
        row == 0,
        ret,
        jnp.where(row == 1, pltpu.roll(ret, 96, 1), jnp.where(row == 2, rhs, pltpu.roll(rhs, 96, 1))),
    )
    extra = jnp.concatenate([extra, jnp.zeros((24, 128), F32)], axis=0)
    lane = iota((32, 128), 1)
    pay_ref[0:64, :] = rsum[0:64]
    pay_ref[64:128, :] = cross_ref[0:64, :]
    pay_ref[128:160, :] = jnp.where(lane < 64, wide[0:32], cross_ref[64:96, :])
    pay_ref[160:192, :] = jnp.where(
        lane // 32 == 1, wide[32:64], jnp.where(lane // 32 == 3, cross_ref[96:128, :], extra)
    )


def eliminate(a):
    rowid = iota((64, 128), 0)
    for k in range(0, K, 4):
        cols = [jnp.broadcast_to(a[:, k + j : k + j + 1], (64, 128)) for j in range(4)]
        rows = [a[k + i : k + i + 1, :] for i in range(4)]
        block = [[cols[j][k + i : k + i + 1, :] for j in range(4)] for i in range(4)]
        for i in range(4):
            inverse = 1.0 / block[i][i]
            rows[i] = rows[i] * inverse
            for j in range(i + 1, 4):
                block[i][j] = block[i][j] * inverse
            for m in range(4):
                if m != i:
                    rows[m] = rows[m] - block[m][i] * rows[i]
                    for j in range(i + 1, 4):
                        block[m][j] = block[m][j] - block[m][i] * block[i][j]
        rest = a
        for i in range(4):
            rest = rest - cols[i] * rows[i]
        for i in range(4):
            rest = jnp.where(rowid == k + i, rows[i], rest)
        a = rest
    return a


def solve_kernel(
    day_ref, side_ref, panel_hbm, pay_ref, near_ref, far_ref, mask_ref, count_ref, coef_ref,
    out_ref, panel_ref, w_ref, sem,
):
    copy = pltpu.make_async_copy(panel_hbm, panel_ref, sem)
    copy.start()
    day = day_ref[0]
    lane = iota((1, 128), 1)
    head = pay_ref[160:168, :]
    moved = pltpu.roll(head, 32, 1)
    ret = jnp.where(lane // 32 % 2 == 0, head[0:1], moved[1:2])
    rhs = jnp.where(lane < 32, head[2:3], moved[3:4])
    r = jnp.concatenate([pay_ref[0:64, :], jnp.broadcast_to(ret, (8, 128))], axis=0)
    top, mid, low = pay_ref[64:128, :], pay_ref[128:160, :], pay_ref[160:192, :]
    wide = iota((32, 128), 1)
    upper = [
        jnp.where(wide >= 64, top[0:32], jnp.where(wide >= 32, mid, 0.0)),
        jnp.where(wide >= 64, top[32:64], 0.0),
        jnp.where(
            wide >= 96, mid, jnp.where((iota((32, 128), 0) == 0) & (wide < 64), rhs, 0.0)
        ),
        jnp.zeros((32, 128), F32),
    ]
    lower = jnp.concatenate(upper, axis=0).T
    cross = jnp.concatenate(
        [
            top,
            jnp.where(wide >= 64, mid, 0.0) + lower[64:96],
            jnp.where(wide >= 96, low, 0.0) + lower[96:128],
        ],
        axis=0,
    )
    gram = jnp.concatenate(
        [
            jnp.where(wide < 64, mid, 0.0) + lower[0:32],
            jnp.where(wide // 32 == 1, low, 0.0) + lower[32:64],
        ],
        axis=0,
    )
    n = count_ref[1:2, 0:128]
    d1 = r / n
    q1 = dot(d1, cross)
    d2 = q1 / n
    q2 = dot(d2, cross)
    d3 = q2 / n
    right = jnp.concatenate([d1 + d2, d2 + d3, d3], axis=1)
    right = jnp.concatenate([right, jnp.zeros((128 - ROWS, 384), F32)], axis=0)
    left = jnp.concatenate([r[0:64], q1[0:64], q2[0:64]], axis=1)
    solved = eliminate(gram - dot_t(left, right))
    coef = jnp.broadcast_to(solved[:, 64:65], (64, 128))
    picked = jnp.where(iota((64, 128), 0) == iota((64, 128), 1), coef, 0.0)
    coef_ref[...] = jnp.sum(picked, axis=0, keepdims=True)[:, 0:K]
    w = jnp.concatenate([-coef, (iota((8, 128), 0) == 0).astype(F32)], axis=0)
    w_ref[...] = w
    e = d1 + d2
    ew = jnp.sum(w * e, axis=0, keepdims=True)
    dw = jnp.sum(w * (e + d3), axis=0, keepdims=True)
    back = lax.dot_general(
        jnp.concatenate(thirds(ew) + [jnp.zeros((13, 128), F32)], axis=0).astype(jnp.bfloat16),
        mask_ref[...].astype(jnp.bfloat16), (((1,), (0,)), ((), ())), preferred_element_type=F32,
    )
    back = back[0:1] + back[1:2] + back[2:3]
    here = iota((8, 128), 1) == 8 * day + iota((8, 128), 0)
    dw = jnp.sum(jnp.where(here, dw, 0.0), axis=1, keepdims=True)
    packed = jnp.zeros((16, 128), F32)
    for q in range(4):
        packed = jnp.where(iota((16, 128), 1) // 32 == q, w[16 * q : 16 * q + 16], packed)
    core = day % 2
    first = 23 * 8 * side_ref[0]

    def part(ref, z):
        row = first + 23 * z + 6
        one = jnp.sum(packed * ref[pl.ds(row, 16), :], axis=0, keepdims=True)
        return one + jnp.where(lane < 32, ref[pl.ds(row + 16, 1), :], 0.0)

    parts = []
    for z in range(8):
        mine, theirs = part(near_ref, z), part(far_ref, z)
        parts += [jnp.where(core == 0, mine, theirs), jnp.where(core == 0, theirs, mine)]
    parts = jnp.concatenate(parts, axis=0)
    parts = parts + pltpu.roll(parts, 32, 1)
    parts = parts + pltpu.roll(parts, 64, 1)
    parts = jnp.where(iota((16, 128), 1) // 32 == iota((16, 128), 0) % 4, parts, 0.0)
    firm = jnp.concatenate(
        [jnp.sum(parts[4 * j : 4 * j + 4], axis=0, keepdims=True) for j in range(4)], axis=1
    )
    firm = back / count_ref[0:1, :] - firm
    mask = mask_ref[pl.ds(pl.multiple_of(day * 8, 8), 8), :]
    copy.wait()
    acc = panel_ref[32 * K : 32 * K + 32, :]
    for c in range(K):
        weight = jnp.broadcast_to(w_ref[c : c + 1, :], (32, 128))
        acc = acc + weight * panel_ref[32 * c : 32 * c + 32, :]
    acc = jnp.concatenate([acc[8 * j : 8 * j + 8] for j in range(4)], axis=1)
    out_ref[...] = mask * (acc + firm - dw)


def call(kernel, out, spaces, scratch, *args):
    kinds = {"s": pltpu.SMEM, "v": pltpu.VMEM, "p": pltpu.VMEM, "h": pl.ANY}
    args = [
        pltpu.with_memory_space_constraint(a, pltpu.VMEM) if s == "v" else a
        for s, a in zip(spaces, args)
    ]
    return pl.pallas_call(
        kernel,
        out_shape=[pltpu.VMEM(s, F32) if v else jax.ShapeDtypeStruct(s, F32) for s, v in out],
        in_specs=[pl.BlockSpec(memory_space=kinds[s]) for s in spaces],
        out_specs=[pl.BlockSpec(memory_space=pltpu.VMEM) for _ in out],
        scratch_shapes=scratch,
    )(*args)


PANEL = pltpu.VMEM((65 * 32, 128), F32)


def sums(day, panel, presence):
    scratch = [PANEL, pltpu.VMEM((8, 512), jnp.int32), pltpu.SemaphoreType.DMA((6,))]
    return call(sums_kernel, [((272, 128), True)], "shh", scratch, day, panel, presence)[0]


def scatter(day, panel, presence, day_n):
    shapes = [((n, 128), True) for n in (ROWS, ROWS, 128, 128)]
    shapes += [((128, 512), True), ((8, 512), True)]
    return call(scatter_kernel, shapes, "sppp", [], day, panel, presence, day_n)


def owner(*args):
    return call(owner_kernel, [((192, 128), True), ((1, 17 * 128), True)], "vvvvv", [], *args)


def solve(*args):
    scratch = [PANEL, pltpu.VMEM((ROWS, 128), F32), pltpu.SemaphoreType.DMA]
    return call(
        solve_kernel, [((1, K), False), ((8, 512), False)], "sshvvvvv", scratch, *args
    )


def exchange(x, axes):
    return lax.all_to_all(x, axes, 0, 0, tiled=True)


def on_device(panel, presence, firm_count, day_count):
    day = lax.axis_index(("z", "c")).astype(jnp.int32).reshape(1)
    side = lax.axis_index("h").astype(jnp.int32).reshape(1)
    panel = panel.reshape(65, 8, 4, 128).transpose(0, 2, 1, 3).reshape(65 * 32, 128)
    msg = exchange(sums(day, panel, presence).reshape(16, 1, 17 * 128), ("z", "c"))
    *here, mask, count = scatter(day, panel, presence, day_count.reshape(1, 128))
    pay, mean = owner(msg.reshape(272, 128), *here)
    pay = jnp.sum(exchange(pay.reshape(32, 1, 6 * 128), ("x", "y", "c")), axis=0)
    near = jnp.concatenate([pay, mean], axis=1).reshape(1, 1, 23 * 128)
    near = exchange(jnp.broadcast_to(near, (16, 1, 23 * 128)), ("h", "z"))
    pay = jnp.sum(near[:, :, : 6 * 128], axis=0)
    far = lax.ppermute(near, "c", ((0, 1), (1, 0)))
    pay = exchange(jnp.broadcast_to(pay[None], (32, 1, 6 * 128)), ("x", "y", "c"))
    pay = pay.reshape(192, 128)
    near, far = near.reshape(368, 128), far.reshape(368, 128)
    coef, residual = solve(day, side, panel, pay, near, far, mask, count)
    return coef.reshape(K), residual


def solution(mesh):
    split = Mesh(mesh.devices.reshape(4, 4, 2, 8, 2), ("x", "y", "h", "z", "c"))
    firm, day = ("x", "y", "h"), ("z", "c")
    return jax.shard_map(
        on_device,
        mesh=split,
        in_specs=(P(None, day, firm), P(None, firm), P(firm), P()),
        out_specs=(P(), P(day, firm)),
        check_vma=False,
    )
```

```python
import jax
import jax.numpy as jnp
from jax import lax
from jax.experimental import pallas as pl
from jax.experimental.pallas import tpu as pltpu
from jax.sharding import Mesh, PartitionSpec as P


K = 64
ROWS = 72
HIGHEST = lax.Precision.HIGHEST
F32 = jnp.float32


def iota(shape, axis):
    return lax.broadcasted_iota(jnp.int32, shape, axis)


def dot_t(a, b):
    return lax.dot_general(
        a, b, (((1,), (1,)), ((), ())), precision=HIGHEST, preferred_element_type=F32
    )


def thirds(a):
    high = a.astype(jnp.bfloat16).astype(F32)
    rest = a - high
    mid = rest.astype(jnp.bfloat16).astype(F32)
    return [high, mid, rest - mid]


def dot(a, b):
    return lax.dot_general(
        a, b, (((1,), (0,)), ((), ())), precision=HIGHEST, preferred_element_type=F32
    )


def stacked(panel_ref, t):
    tiles = []
    for j in range(4):
        row = 8 * j + t
        target = panel_ref[32 * K + row : 32 * K + row + 1, :]
        regress = panel_ref[pl.ds(row, K, stride=32), :]
        tiles.append(jnp.concatenate([regress, jnp.broadcast_to(target, (8, 128))], axis=0))
    return jnp.concatenate(tiles, axis=1)


def sums_kernel(day_ref, panel_hbm, pres_hbm, msg_ref, panel_ref, pres_ref, sems):
    start = pl.multiple_of(day_ref[0] * 8, 8)
    copies = [pltpu.make_async_copy(pres_hbm.at[pl.ds(start, 8), :], pres_ref, sems.at[0])]
    pieces = [slice(512 * q, 512 * q + 512) for q in range(4)] + [slice(32 * K, 32 * K + 32)]
    for i, rows in enumerate(pieces):
        copies.append(
            pltpu.make_async_copy(panel_hbm.at[rows, :], panel_ref.at[rows, :], sems.at[i + 1])
        )
    for copy in copies:
        copy.start()
    copies[0].wait()
    mask = pres_ref[...].astype(F32)
    low = [iota((8, 128), 0) % (2 * n) < n for n in (4, 2, 1)]
    for q in range(4):
        copies[q + 1].wait()
        tiles = []
        for j in range(4):
            held = mask[:, 128 * j : 128 * j + 128]
            halves = []
            for half in range(2):
                base = 512 * q + 256 * half + 8 * j
                rows = [base + 32 * c for c in (0, 4, 2, 6, 1, 5, 3, 7)]
                level = [panel_ref[r : r + 8, :] * held for r in rows]
                for n, mine in zip((4, 2, 1), low):
                    level = [
                        jnp.where(mine, x + pltpu.roll(x, 8 - n, 0), y + pltpu.roll(y, n, 0))
                        for x, y in zip(level[0::2], level[1::2])
                    ]
                halves.append(level[0])
            tiles.append(jnp.concatenate(halves, axis=0))
        for d in range(16):
            lanes = slice(32 * (d % 4), 32 * (d % 4) + 32)
            msg_ref[17 * d : 17 * d + 16, 32 * q : 32 * q + 32] = tiles[d // 4][:, lanes]
    copies[5].wait()
    for j in range(4):
        x = panel_ref[32 * K + 8 * j : 32 * K + 8 * j + 8, :] * mask[:, 128 * j : 128 * j + 128]
        total = jnp.sum(x, axis=0, keepdims=True)
        for s in range(4):
            d = 4 * j + s
            msg_ref[17 * d + 16 : 17 * d + 17, :] = jnp.zeros((1, 128), F32)
            msg_ref[17 * d + 16 : 17 * d + 17, 0:32] = total[:, 32 * s : 32 * s + 32]


def scatter_kernel(
    day_ref, panel_ref, pres_ref, dayn_ref, gram_ref, rsum_ref, own_ref, cross_ref, mask_ref, count_ref
):
    day = day_ref[0]
    every = pres_ref[...].astype(F32)
    mask_ref[...] = every
    firm_n = jnp.sum(every, axis=0, keepdims=True)
    day_n = jnp.concatenate([dayn_ref[...].astype(F32), jnp.zeros((1, 384), F32)], axis=1)
    count_ref[...] = jnp.concatenate([firm_n, day_n, jnp.zeros((6, 512), F32)], axis=0)
    mask = mask_ref[pl.ds(pl.multiple_of(day * 8, 8), 8), :]
    count = jnp.sum(mask, axis=0, keepdims=True)
    total = mask[0:1] * stacked(panel_ref, 0)
    for t in range(1, 8):
        total = total + mask[t : t + 1] * stacked(panel_ref, t)
    mean = total / jnp.maximum(count, 1.0)
    gram = jnp.zeros((ROWS, ROWS), F32)
    rsum = jnp.zeros((ROWS, 128), F32)
    lane = iota((ROWS, 128), 1)
    for t in range(8):
        centred = mask[t : t + 1] * (stacked(panel_ref, t) - mean)
        gram = gram + dot_t(centred, centred)
        sums = jnp.sum(centred, axis=1, keepdims=True)
        rsum = rsum + jnp.where(lane == 8 * day + t, sums, 0.0)
    gram_ref[...] = jnp.concatenate([gram, jnp.zeros((ROWS, 128 - ROWS), F32)], axis=1)
    rsum_ref[...] = rsum
    pick = (iota((512, 128), 0) == 32 * day + iota((512, 128), 1) % 32).astype(jnp.bfloat16)
    own = lax.dot_general(
        every.astype(jnp.bfloat16), pick, (((1,), (0,)), ((), ())),
        preferred_element_type=F32,
    )
    own_ref[...] = own
    firm_n = jnp.sum(own, axis=0, keepdims=True)
    weight = jnp.where(iota((1, 128), 1) < 32, 1.0 / firm_n, 0.0)
    cross_ref[...] = dot_t(own * weight, own)


def owner_kernel(msg_ref, gram_ref, rsum_ref, own_ref, cross_ref, pay_ref, mean_ref):
    own = own_ref[...]
    per_block = jnp.sum(own.reshape(16, 8, 128), axis=1)
    firm_n = jnp.sum(per_block, axis=0, keepdims=True)
    msg = [msg_ref[17 * b : 17 * b + 16, :] for b in range(16)]
    last = jnp.concatenate([msg_ref[17 * b + 16 : 17 * b + 17, :] for b in range(16)], axis=0)
    total = msg[0]
    for b in range(1, 16):
        total = total + msg[b]
    mean = total / firm_n
    last_mean = jnp.sum(last, axis=0, keepdims=True) / firm_n
    for k in range(16):
        mean_ref[:, 128 * k : 128 * k + 128] = mean[k : k + 1]
    mean_ref[:, 2048:2176] = last_mean
    held = jnp.maximum(per_block, 1.0)
    delta = [msg[b] / held[b : b + 1] - mean for b in range(16)]
    last = last / held - last_mean

    gram = gram_ref[:, 0:ROWS]
    rsum = rsum_ref[...]
    block = iota((128, 128), 0) // 8
    group = iota((128, 128), 1) // 32
    for j in range(4):
        rows = [
            jnp.concatenate([delta[4 * j + s][:, 32 * q : 32 * q + 32] for s in range(4)], axis=1)
            for q in range(4)
        ]
        ret = jnp.concatenate([last[4 * j + s : 4 * j + s + 1, 0:32] for s in range(4)], axis=1)
        rows.append(jnp.broadcast_to(ret, (8, 128)))
        spread = jnp.concatenate(rows, axis=0)
        cells = jnp.where(block == 4 * j + group, own, 0.0)
        weight = jnp.sum(cells, axis=0, keepdims=True)
        gram = gram + dot_t(spread * weight, spread)
        three = jnp.concatenate(thirds(spread) + [jnp.zeros((8, 128), F32)], axis=0)
        sums = lax.dot_general(
            three.astype(jnp.bfloat16), cells.astype(jnp.bfloat16), (((1,), (1,)), ((), ())),
            preferred_element_type=F32,
        )
        rsum = rsum + (sums[0:72] + sums[72:144] + sums[144:216])
    wide = jnp.concatenate([gram, jnp.zeros((ROWS, 128 - ROWS), F32)], axis=1)
    ret, rhs, row = rsum[64:72], wide[64:72], iota((8, 128), 0)
    extra = jnp.where(
        row == 0,
        ret,
        jnp.where(row == 1, pltpu.roll(ret, 96, 1), jnp.where(row == 2, rhs, pltpu.roll(rhs, 96, 1))),
    )
    extra = jnp.concatenate([extra, jnp.zeros((24, 128), F32)], axis=0)
    lane = iota((32, 128), 1)
    pay_ref[0:64, :] = rsum[0:64]
    pay_ref[64:128, :] = cross_ref[0:64, :]
    pay_ref[128:160, :] = jnp.where(lane < 64, wide[0:32], cross_ref[64:96, :])
    pay_ref[160:192, :] = jnp.where(
        lane // 32 == 1, wide[32:64], jnp.where(lane // 32 == 3, cross_ref[96:128, :], extra)
    )


def eliminate(a):
    rowid = iota((64, 128), 0)
    for k in range(0, K, 4):
        cols = [jnp.broadcast_to(a[:, k + j : k + j + 1], (64, 128)) for j in range(4)]
        rows = [a[k + i : k + i + 1, :] for i in range(4)]
        block = [[cols[j][k + i : k + i + 1, :] for j in range(4)] for i in range(4)]
        for i in range(4):
            inverse = 1.0 / block[i][i]
            rows[i] = rows[i] * inverse
            for j in range(i + 1, 4):
                block[i][j] = block[i][j] * inverse
            for m in range(4):
                if m != i:
                    rows[m] = rows[m] - block[m][i] * rows[i]
                    for j in range(i + 1, 4):
                        block[m][j] = block[m][j] - block[m][i] * block[i][j]
        rest = a
        for i in range(4):
            rest = rest - cols[i] * rows[i]
        for i in range(4):
            rest = jnp.where(rowid == k + i, rows[i], rest)
        a = rest
    return a


def solve_kernel(
    day_ref, side_ref, panel_hbm, pay_ref, near_ref, far_ref, mask_ref, count_ref, coef_ref,
    out_ref, panel_ref, w_ref, sem,
):
    copy = pltpu.make_async_copy(panel_hbm, panel_ref, sem)
    copy.start()
    day = day_ref[0]
    lane = iota((1, 128), 1)
    head = pay_ref[160:168, :]
    moved = pltpu.roll(head, 32, 1)
    ret = jnp.where(lane // 32 % 2 == 0, head[0:1], moved[1:2])
    rhs = jnp.where(lane < 32, head[2:3], moved[3:4])
    r = jnp.concatenate([pay_ref[0:64, :], jnp.broadcast_to(ret, (8, 128))], axis=0)
    top, mid, low = pay_ref[64:128, :], pay_ref[128:160, :], pay_ref[160:192, :]
    wide = iota((32, 128), 1)
    upper = [
        jnp.where(wide >= 64, top[0:32], jnp.where(wide >= 32, mid, 0.0)),
        jnp.where(wide >= 64, top[32:64], 0.0),
        jnp.where(
            wide >= 96, mid, jnp.where((iota((32, 128), 0) == 0) & (wide < 64), rhs, 0.0)
        ),
        jnp.zeros((32, 128), F32),
    ]
    lower = jnp.concatenate(upper, axis=0).T
    cross = jnp.concatenate(
        [
            top,
            jnp.where(wide >= 64, mid, 0.0) + lower[64:96],
            jnp.where(wide >= 96, low, 0.0) + lower[96:128],
        ],
        axis=0,
    )
    gram = jnp.concatenate(
        [
            jnp.where(wide < 64, mid, 0.0) + lower[0:32],
            jnp.where(wide // 32 == 1, low, 0.0) + lower[32:64],
        ],
        axis=0,
    )
    n = count_ref[1:2, 0:128]
    d1 = r / n
    q1 = dot(d1, cross)
    d2 = q1 / n
    q2 = dot(d2, cross)
    d3 = q2 / n
    right = jnp.concatenate([d1 + d2, d2 + d3, d3], axis=1)
    right = jnp.concatenate([right, jnp.zeros((128 - ROWS, 384), F32)], axis=0)
    left = jnp.concatenate([r[0:64], q1[0:64], q2[0:64]], axis=1)
    solved = eliminate(gram - dot_t(left, right))
    coef = jnp.broadcast_to(solved[:, 64:65], (64, 128))
    picked = jnp.where(iota((64, 128), 0) == iota((64, 128), 1), coef, 0.0)
    coef_ref[...] = jnp.sum(picked, axis=0, keepdims=True)[:, 0:K]
    w = jnp.concatenate([-coef, (iota((8, 128), 0) == 0).astype(F32)], axis=0)
    w_ref[...] = w
    e = d1 + d2
    ew = jnp.sum(w * e, axis=0, keepdims=True)
    dw = jnp.sum(w * (e + d3), axis=0, keepdims=True)
    back = dot(jnp.broadcast_to(ew, (8, 128)), mask_ref[...])[0:1]
    here = iota((8, 128), 1) == 8 * day + iota((8, 128), 0)
    dw = jnp.sum(jnp.where(here, dw, 0.0), axis=1, keepdims=True)
    packed = jnp.zeros((16, 128), F32)
    for q in range(4):
        packed = jnp.where(iota((16, 128), 1) // 32 == q, w[16 * q : 16 * q + 16], packed)
    core = day % 2
    first = 23 * 8 * side_ref[0]

    def part(ref, z):
        row = first + 23 * z + 6
        one = jnp.sum(packed * ref[pl.ds(row, 16), :], axis=0, keepdims=True)
        return one + jnp.where(lane < 32, ref[pl.ds(row + 16, 1), :], 0.0)

    parts = []
    for z in range(8):
        mine, theirs = part(near_ref, z), part(far_ref, z)
        parts += [jnp.where(core == 0, mine, theirs), jnp.where(core == 0, theirs, mine)]
    parts = jnp.concatenate(parts, axis=0)
    parts = parts + pltpu.roll(parts, 32, 1)
    parts = parts + pltpu.roll(parts, 64, 1)
    parts = jnp.where(iota((16, 128), 1) // 32 == iota((16, 128), 0) % 4, parts, 0.0)
    firm = jnp.concatenate(
        [jnp.sum(parts[4 * j : 4 * j + 4], axis=0, keepdims=True) for j in range(4)], axis=1
    )
    firm = back / count_ref[0:1, :] - firm
    mask = mask_ref[pl.ds(pl.multiple_of(day * 8, 8), 8), :]
    copy.wait()
    acc = panel_ref[32 * K : 32 * K + 32, :]
    for c in range(K):
        weight = jnp.broadcast_to(w_ref[c : c + 1, :], (32, 128))
        acc = acc + weight * panel_ref[32 * c : 32 * c + 32, :]
    acc = jnp.concatenate([acc[8 * j : 8 * j + 8] for j in range(4)], axis=1)
    out_ref[...] = mask * (acc + firm - dw)


def call(kernel, out, spaces, scratch, *args):
    kinds = {"s": pltpu.SMEM, "v": pltpu.VMEM, "p": pltpu.VMEM, "h": pl.ANY}
    args = [
        pltpu.with_memory_space_constraint(a, pltpu.VMEM) if s == "v" else a
        for s, a in zip(spaces, args)
    ]
    return pl.pallas_call(
        kernel,
        out_shape=[pltpu.VMEM(s, F32) if v else jax.ShapeDtypeStruct(s, F32) for s, v in out],
        in_specs=[pl.BlockSpec(memory_space=kinds[s]) for s in spaces],
        out_specs=[pl.BlockSpec(memory_space=pltpu.VMEM) for _ in out],
        scratch_shapes=scratch,
    )(*args)


PANEL = pltpu.VMEM((65 * 32, 128), F32)


def sums(day, panel, presence):
    scratch = [PANEL, pltpu.VMEM((8, 512), jnp.int32), pltpu.SemaphoreType.DMA((6,))]
    return call(sums_kernel, [((272, 128), True)], "shh", scratch, day, panel, presence)[0]


def scatter(day, panel, presence, day_n):
    shapes = [((n, 128), True) for n in (ROWS, ROWS, 128, 128)]
    shapes += [((128, 512), True), ((8, 512), True)]
    return call(scatter_kernel, shapes, "sppp", [], day, panel, presence, day_n)


def owner(*args):
    return call(owner_kernel, [((192, 128), True), ((1, 17 * 128), True)], "vvvvv", [], *args)


def solve(*args):
    scratch = [PANEL, pltpu.VMEM((ROWS, 128), F32), pltpu.SemaphoreType.DMA]
    return call(
        solve_kernel, [((1, K), False), ((8, 512), False)], "sshvvvvv", scratch, *args
    )


def exchange(x, axes):
    return lax.all_to_all(x, axes, 0, 0, tiled=True)


def on_device(panel, presence, firm_count, day_count):
    day = lax.axis_index(("z", "c")).astype(jnp.int32).reshape(1)
    side = lax.axis_index("h").astype(jnp.int32).reshape(1)
    panel = panel.reshape(65, 8, 4, 128).transpose(0, 2, 1, 3).reshape(65 * 32, 128)
    msg = exchange(sums(day, panel, presence).reshape(16, 1, 17 * 128), ("z", "c"))
    *here, mask, count = scatter(day, panel, presence, day_count.reshape(1, 128))
    pay, mean = owner(msg.reshape(272, 128), *here)
    pay = jnp.sum(exchange(pay.reshape(32, 1, 6 * 128), ("x", "y", "c")), axis=0)
    near = jnp.concatenate([pay, mean], axis=1).reshape(1, 1, 23 * 128)
    near = exchange(jnp.broadcast_to(near, (16, 1, 23 * 128)), ("h", "z"))
    pay = jnp.sum(near[:, :, : 6 * 128], axis=0)
    far = lax.ppermute(near, "c", ((0, 1), (1, 0)))
    pay = exchange(jnp.broadcast_to(pay[None], (32, 1, 6 * 128)), ("x", "y", "c"))
    pay = pay.reshape(192, 128)
    near, far = near.reshape(368, 128), far.reshape(368, 128)
    coef, residual = solve(day, side, panel, pay, near, far, mask, count)
    return coef.reshape(K), residual


def solution(mesh):
    split = Mesh(mesh.devices.reshape(4, 4, 2, 8, 2), ("x", "y", "h", "z", "c"))
    firm, day = ("x", "y", "h"), ("z", "c")
    return jax.shard_map(
        on_device,
        mesh=split,
        in_specs=(P(None, day, firm), P(None, firm), P(firm), P()),
        out_specs=(P(), P(day, firm)),
        check_vma=False,
    )
```
